32 devices in a mesh: row: 2 (over core), blk: 16 (over z, y, x).
Axes of the slice: x: 2, y: 2, z: 4, core: 2. Of those that a mesh axis runs over, the one named last changes fastest.
Arguments:
- state: float32 [2, 5, 512, 512], P('row', None, 'blk'), may hold values from -6 to 6
- forcing: float32 [2, 5, 512, 512], P('row', None, 'blk'), may hold values from -6 to 6
- sigma: float32 [2, 512, 512], P('row', 'blk'), may hold values from 0.05 to 2
- partner: int32 [2, 512, 1], P('row', 'blk'), may hold values from 0 to 15; in each aligned block of 32 rows (0 to 31, 32 to 63, ..., all dimensions but the last counted through in order) at most 4 rows name the same one
- loop_weight: float32 [2, 128], P('row'), may hold values from 0.05 to 0.2
- offset: int32 [1], replicated, may hold values from 0 to 127
Outputs:
- solution: float32 [2, 5, 512, 512], P('row', None, 'blk')
- loop_correction: float32 [2, 5, 128], P('row', None, 'blk')
The draws below stay inside these ranges and needn't reach their ends.
Inputs may be any that keep to these rules, and one draw needn't show every extreme that they name: Among the 32 face cells of one device no partner slot is named more than 4 times.
All inputs are finite; a program needn't handle non-finite values.
Results may differ from the reference program's by a relative error of at most 0.00011.
Values sent between devices are 32-bit elements; how exact they have to be, the bound alone decides.
No kernel may reach another device: no remote copies, remote signals or barrier semaphores. Data moves between devices by JAX's collectives and lax.ppermute only.
A program may use at most 64 MiB of HBM per device.

```python
import math
import jax
import jax.numpy as jnp
import numpy as np

V = 5
CI = 32
CJ = 512
SECTIONS1 = 3
SECTIONS2 = 3
SECTIONS3 = 4
MOST = 4
LOOP_SLOTS = 16
NI = 512
NRING = 128


def shard_levels(rng, dims, cuts, least, largest):
    loudness, own = 1.0, jax.random.fold_in(rng, 6)
    for position, blocks in cuts:
        draws = jnp.exp(jax.random.uniform(jax.random.fold_in(own, position), (blocks,), jnp.float32, least / len(cuts), largest / len(cuts)))
        loudness = loudness * jnp.repeat(draws, dims[position] // blocks).reshape([-1 if axis == position else 1 for axis in range(len(dims))])
    return loudness


def shared_out(stream_key, own, number, rows, amount, top, reach, slope):
    ranking = jax.random.permutation(stream_key, amount)
    heavy_load, common = load_shares(amount, rows * top, reach, slope, True), load_shares(amount, rows * top, reach, slope, False)
    places = jnp.arange(amount)

    def named(lengths, offset_by):
        used = int((lengths > 0).sum())
        fixed = max(1, used // 4)
        passed = fixed + (places - fixed + offset_by * (used - fixed)) % max(1, amount - fixed)
        return jnp.zeros((amount,), jnp.int32).at[ranking[jnp.where(places < fixed, places, passed)]].set(jnp.asarray(lengths, jnp.int32))

    lengths = jnp.where(number % 4 == 0, named(heavy_load, number // 4), named(common, number - number // 4 - 1))
    mixed = jax.random.permutation(jax.random.fold_in(own, 3), amount)
    donor, taker = mixed[0:amount // 2 * 2:2], mixed[1:amount // 2 * 2:2]
    margin = jnp.minimum(lengths[donor] - 1, reach - lengths[taker]) // 2
    margin = jnp.where((donor == ranking[0]) | (taker == ranking[0]) | (lengths[taker] == 0), 0, jnp.maximum(margin, 0))
    passed = jax.random.randint(jax.random.fold_in(own, 4), (amount // 2,), 0, 1 << 20) % (margin + 1)
    lengths = lengths.at[donor].add(-passed).at[taker].add(passed)
    members = jnp.searchsorted(jnp.cumsum(lengths), jnp.arange(rows * top), side="right").astype(jnp.int32)
    grid = members.reshape(top, rows).T
    grid = grid[jax.random.permutation(jax.random.fold_in(own, 1), rows)]
    offset_by = jax.random.randint(jax.random.fold_in(own, 2), (rows, 1), 0, top)
    return jnp.take_along_axis(grid, (jnp.arange(top)[None, :] + offset_by) % top, axis=1)


def load_shares(count, total, bound, slope, full):
    portions = [(1 << 20) // math.isqrt(grade ** slope) + 1 for grade in range(1, count + 1)]
    largest = bound if full else min(bound, max(-(-total // count), total * portions[0] // sum(portions)))
    least = 1 if total - largest >= count - 1 else 0
    counts, rest = [largest] + [least] * (count - 1), total - largest - least * (count - 1)
    while rest > 0:
        candidates = [i for i in range(1, count) if counts[i] < largest] or [i for i in range(1, count) if counts[i] < bound]
        mass, left = sum([portions[i] for i in candidates]), rest
        for i in candidates:
            more = min(bound - counts[i], max(1, left * portions[i] // mass), rest)
            counts[i] = counts[i] + more
            rest = rest - more
    return np.array(counts)


def scatter_about(own_key, dims, deviation, limit, split=(), held_as=jnp.bfloat16):
    entries = deviation * jax.random.normal(own_key, dims, jnp.float32)
    if split:
        entries = entries * shard_levels(own_key, dims, split, -0.22, 0.18)
    return jnp.clip(entries, -limit, limit).astype(held_as)


def setup_inputs(seed: int = 0) -> dict:
    seeds = jax.random.split(jax.random.key(seed), 7)
    state = scatter_about(seeds[0], (2, V, NI, CJ), 1.0, 6.0, ((0, 2), (2, 16)), jnp.float32)
    forcing = scatter_about(seeds[1], (2, V, NI, CJ), 1.0, 6.0, ((0, 2), (2, 16)), jnp.float32)
    sigma = jnp.clip(jnp.exp(math.log(2.0) - 3.6888794 * jax.random.uniform(seeds[2], (2, NI, CJ), jnp.float32) ** shard_levels(seeds[2], (2, NI, CJ), ((0, 2), (1, 16)), -0.2, 0.2)), 0.05, 2.0)
    partner_keys = jax.random.split(jax.random.fold_in(seeds[3], 1), 2 * NI // CI)
    partner_turns = jax.random.permutation(jax.random.fold_in(seeds[3], 3), 2 * NI // CI)
    partner = jax.vmap(lambda own, number: shared_out(jax.random.fold_in(seeds[3], 2), own, number, CI, LOOP_SLOTS, 1, MOST, 2))(partner_keys, partner_turns).reshape((2, NI, 1))
    loop_weight = jnp.clip(jnp.exp(math.log(0.2) - 1.3862944 * jax.random.uniform(seeds[4], (2, NRING), jnp.float32) ** shard_levels(seeds[4], (2, NRING), ((0, 2),), -0.2, 0.2)), 0.05, 0.2)
    offset = jax.random.randint(seeds[5], (1,), 0, NRING).astype(jnp.int32)
    return dict(state=state, forcing=forcing, sigma=sigma, partner=partner, loop_weight=loop_weight, offset=offset)


COEFF = 0.8


def nonlinear(field):
    q = jnp.mean(field * field, axis=0, keepdims=True)
    return 0.5 * field * q / (1.0 + q)


def operator(field, sigma_in, scale):
    across = jnp.roll(field, 1, axis=1) + jnp.roll(field, -1, axis=1)
    padded = jnp.pad(field, ((0, 0), (0, 0), (1, 1)))
    along = padded[:, :, 2:] + padded[:, :, :-2]
    return scale * (4.0 * field - (across + along)) + sigma_in[None] * field + nonlinear(field)


def smooth(field, source, sigma_in, scale, count):
    tau = (COEFF / (4.0 * scale + sigma_in + 1.5))[None]
    start = field
    for section in range(count):
        field = start + (1.0 / (count - section)) * tau * (source - operator(field, sigma_in, scale))
    return field


def coarsen(x):
    rows, cols = x.shape[-2], x.shape[-1]
    return x.reshape(x.shape[:-2] + (rows // 2, 2, cols // 2, 2)).mean(axis=(-3, -1))


def refine(x):
    return jnp.repeat(jnp.repeat(x, 2, axis=-2), 2, axis=-1)


def loop_cells_of(partner_row):
    blocks = NI // CI
    owner_block = (jnp.arange(NI, dtype=jnp.int32) // CI).astype(jnp.int32)
    return ((partner_row * blocks + owner_block) % NRING).astype(jnp.int32)


def reference(state, forcing, sigma, partner, loop_weight, offset):
    fine_states = []
    fine_resid = []
    sums = []
    cells = []
    for row in range(2):
        u1 = smooth(state[row], forcing[row], sigma[row], 1.0, SECTIONS1)
        r1 = forcing[row] - operator(u1, sigma[row], 1.0)
        if row == 0:
            face = r1[:, :, -1]
        else:
            face = r1[:, :, 0]
        loop_cell = loop_cells_of(partner[row, :, 0])
        cells.append(loop_cell)
        sums.append(jax.ops.segment_sum(face.T, loop_cell, num_segments=NRING).T)
        fine_states.append(u1)
        fine_resid.append(r1)
    shift = offset[0]
    corr_rotor = loop_weight[0][None, :] * (sums[0] + jnp.roll(sums[1], -shift, axis=1))
    corr_stator = loop_weight[1][None, :] * (sums[1] + jnp.roll(sums[0], shift, axis=1))
    corrections = [corr_rotor, corr_stator]
    results = []
    for row in range(2):
        u1 = fine_states[row]
        r1 = fine_resid[row]
        s1 = sigma[row]
        s2 = coarsen(s1)
        s3 = coarsen(s2)
        u2_start = coarsen(u1)
        f2 = operator(u2_start, s2, 0.25) + coarsen(r1)
        u2 = smooth(u2_start, f2, s2, 0.25, SECTIONS2)
        r2 = f2 - operator(u2, s2, 0.25)
        u3_start = coarsen(u2)
        f3 = operator(u3_start, s3, 0.0625) + coarsen(r2)
        u3 = smooth(u3_start, f3, s3, 0.0625, SECTIONS3)
        u2 = u2 + refine(u3 - u3_start)
        u2 = smooth(u2, f2, s2, 0.25, SECTIONS2)
        u1 = u1 + refine(u2 - u2_start)
        fix = corrections[row][:, cells[row]]
        column = CJ - 1 if row == 0 else 0
        u1 = u1.at[:, :, column].add(fix)
        u1 = smooth(u1, forcing[row], s1, 1.0, SECTIONS1)
        results.append(u1)
    return jnp.stack(results), jnp.stack(corrections)
```

```python
import functools

import jax
import jax.numpy as jnp
from jax import lax
from jax.experimental import pallas as pl
from jax.experimental.pallas import tpu as pltpu
from jax.sharding import PartitionSpec as P

SECTIONS1 = 3
SECTIONS2 = 3
SECTIONS3 = 4
COEFF = 0.8

FOLD = 4


def vmem():
    return pl.BlockSpec(memory_space=pltpu.VMEM)


def lanes_of(rows, cols):
    return lax.broadcasted_iota(jnp.int32, (rows, cols), 1)


def rows_of(rows, cols):
    return lax.broadcasted_iota(jnp.int32, (rows, cols), 0)


def pick(x, index):
    return jnp.take_along_axis(x, index, axis=1, mode="promise_in_bounds")


def split_lanes(x):
    rows, cols = x.shape
    wide = cols // FOLD
    run = wide // FOLD
    lane = lanes_of(rows, wide)
    parts = [x[:, c * wide : (c + 1) * wide] for c in range(FOLD)]
    group = lane // run
    out = []
    for b in range(FOLD):
        index = (lane % run) * FOLD + b
        taken = [pick(p, index) for p in parts]
        value = taken[-1]
        for c in range(FOLD - 1):
            value = jnp.where(group == c, taken[c], value)
        out.append(value)
    return out


def join_lanes(parts):
    rows, wide = parts[0].shape
    run = wide // FOLD
    lane = lanes_of(rows, wide)
    turn = lane % FOLD
    out = []
    for c in range(FOLD):
        index = lane // FOLD + c * run
        taken = [pick(p, index) for p in parts]
        value = taken[-1]
        for b in range(FOLD - 1):
            value = jnp.where(turn == b, taken[b], value)
        out.append(value)
    return out


def residual(src, source, diag, scale, a, b, fold, rows):
    count = src.shape[0]
    total, wide = src.shape[-2:]
    u = [src[v, a, b][:rows] for v in range(count)]
    q = u[0] * u[0]
    for v in range(1, count):
        q = q + u[v] * u[v]
    q = q * (1.0 / count)
    factor = diag + 0.5 * q / (1.0 + q)
    lane = lanes_of(rows, wide)
    out = []
    for v in range(count):
        up = src[v, a - 1, b] if a else pltpu.roll(src[v, fold - 1, b], 1, 0)
        down = src[v, a + 1, b] if a < fold - 1 else pltpu.roll(src[v, 0, b], total - 1, 0)
        if b:
            left = src[v, a, b - 1][:rows]
        else:
            left = jnp.where(lane == 0, 0.0, pltpu.roll(src[v, a, fold - 1][:rows], 1, 1))
        if b < fold - 1:
            right = src[v, a, b + 1][:rows]
        else:
            right = jnp.where(lane == wide - 1, 0.0, pltpu.roll(src[v, a, 0][:rows], wide - 1, 1))
        near = (up[:rows] + down[:rows]) + (left + right)
        out.append(source[v, a, b][:rows] + scale * near - factor * u[v])
    return out


def section(dst, src, start, source, sigma, scale, weight, fold, rows):
    for a in range(fold):
        for b in range(fold):
            diag = 4.0 * scale + sigma[a, b][:rows]
            step = weight * (COEFF / (diag + 1.5))
            res = residual(src, source, diag, scale, a, b, fold, rows)
            for v, r in enumerate(res):
                dst[v, a, b, :rows] = start[v, a, b][:rows] + step * r


def first_section(dst, start, coarse, sigma, scale, weight, fold):
    for a in range(fold):
        for b in range(fold):
            step = weight * (COEFF / (4.0 * scale + sigma[a, b] + 1.5))
            for v in range(dst.shape[0]):
                dst[v, a, b] = start[v, a, b] + step * coarse[v, a, b]


def quarter(x):
    return 0.25 * ((x(0, 0) + x(0, 1)) + (x(1, 0) + x(1, 1)))


def wrap(x, size):
    return x & (size - 1) if size & (size - 1) == 0 else lax.rem(x, size)


def pack_kernel(s_head, s_tail, f_head, f_tail, g_head, g_tail, p_ref, head, tail):
    count = s_head.shape[1]
    rows = p_ref.shape[1]
    cols = head.shape[1]
    edge = FOLD
    deep = s_tail.shape[2]
    for v in range(count):
        for k, (top, bottom) in enumerate(((s_head, s_tail), (f_head, f_tail))):
            at = (k * count + v) * edge
            head[at : at + edge] = top[0, v, :edge]
            tail[at : at + edge] = bottom[0, v, deep - edge :]
    at = 2 * count * edge
    head[at : at + edge] = g_head[0, :edge]
    tail[at : at + edge] = g_tail[0, deep - edge :]
    at += edge
    head[at : at + edge] = jnp.broadcast_to(p_ref[0, :edge].astype(jnp.float32), (edge, cols))
    tail[at : at + edge] = jnp.broadcast_to(p_ref[0, rows - edge :].astype(jnp.float32), (edge, cols))


def fold_kernel(s_ref, f_ref, g_ref, st, fo, sg, stage):
    rows = st.shape[-2]
    count = st.shape[0]
    for ch in range(2 * count + 1):
        kind, v = divmod(ch, count)
        x = g_ref[0] if kind == 2 else (s_ref, f_ref)[kind][0, v]
        for b, part in enumerate(split_lanes(x)):
            stage[ch, b] = part
        for a in range(FOLD):
            for b in range(FOLD):
                part = stage[ch, b, pl.ds(a, rows, stride=FOLD), :]
                if kind == 2:
                    sg[a, b] = part
                else:
                    (st, fo)[kind][v, a, b] = part


def down_kernel(
    st, fo, sg, below, above, p_ref,
    u1, source, sigma, cells, head, tail, loop,
    start, buf_a, buf_b, edge_buf, resid, own_slot,
):
    count = st.shape[0]
    R, J = st.shape[-2:]
    N = loop.shape[1]
    edge = FOLD
    row = lax.axis_index("row")
    blk = lax.axis_index("blk")
    blocks = lax.axis_size("blk")
    sub = rows_of(R, J)
    for ch in range(2 * count + 1):
        x = jnp.concatenate(
            [below[ch * edge : (ch + 1) * edge], above[ch * edge : (ch + 1) * edge]], axis=0
        )
        for b, part in enumerate(split_lanes(x)):
            edge_buf[ch, b] = part

    def halo(ch, a, b):
        low = edge_buf[ch, b, a : a + 1]
        high = edge_buf[ch, b, edge + a : edge + a + 1]
        return jnp.where(sub == 0, high, jnp.where(sub == R - 1, low, 0.0))

    own_slot[...] = jnp.broadcast_to(p_ref[0], own_slot.shape)
    for a in range(FOLD):
        for b in range(FOLD):
            for v in range(count):
                start[v, a, b, :R] = st[v, a, b]
                start[v, a, b, R:] = halo(v, a, b)
                source[v, a, b, :R] = fo[v, a, b]
                source[v, a, b, R:] = halo(count + v, a, b)
            sigma[a, b, :R] = sg[a, b]
            sigma[a, b, R:] = halo(2 * count, a, b)
        at = (2 * count + 1) * edge + a
        own = own_slot[pl.ds(a, R, stride=FOLD), :]
        low = below[at : at + 1, :J].astype(jnp.int32)
        high = above[at : at + 1, :J].astype(jnp.int32)
        cells[a, :R] = wrap(own * blocks + blk, N)
        cells[a, R:] = jnp.where(
            sub < R // 2,
            wrap(high * blocks + lax.rem(blk + 1, blocks), N),
            wrap(low * blocks + lax.rem(blk + blocks - 1, blocks), N),
        )

    src = start
    for k in range(SECTIONS1):
        dst = (buf_a, buf_b)[k % 2]
        section(dst, src, start, source, sigma, 1.0, 1.0 / (SECTIONS1 - k), FOLD, 2 * R)
        src = dst

    for a in range(FOLD):
        for b in range(FOLD):
            res = residual(src, source, 4.0 + sigma[a, b][:R], 1.0, a, b, FOLD, R)
            for v in range(count):
                resid[v, a, b] = res[v]
                u = src[v, a, b][:R]
                u1[v, a, b] = u
                at = (v * FOLD + a) * FOLD + b
                k = (2 * count + 1) * 4 + at // R
                head[k, at % R : at % R + 1] = u[:1]
                tail[k, at % R : at % R + 1] = u[R - 1 :]
    for a in range(2):
        for b in range(2):
            for v in range(count):
                at = (v * 2 + a) * 2 + b
                x = quarter(lambda i, j: u1[v, 2 * a + i, 2 * b + j])
                head[at] = x
                tail[at] = x
                at += 4 * count
                x = quarter(lambda i, j: resid[v, 2 * a + i, 2 * b + j])
                head[at] = x
                tail[at] = x
            at = 8 * count + a * 2 + b
            x = quarter(lambda i, j: sg[2 * a + i, 2 * b + j])
            head[at] = x
            tail[at] = x

    lane = lanes_of(R, J)
    ring = lanes_of(R, N)
    sums = [jnp.zeros((R, N), jnp.float32) for _ in range(count)]
    column = jnp.where(row == 0, J - 1, 0)
    for a in range(FOLD):
        match = cells[a, :R, :1] == ring
        for v in range(count):
            face = jnp.where(row == 0, resid[v, a, FOLD - 1], resid[v, a, 0])
            face = jnp.sum(jnp.where(lane == column, face, 0.0), axis=1, keepdims=True)
            sums[v] = sums[v] + jnp.where(match, face, 0.0)
    loop[...] = jnp.zeros_like(loop)
    half = loop.shape[0] // 2
    for v in range(count):
        total = jnp.sum(sums[v], axis=0, keepdims=True)
        for r in range(2):
            at = r * half + v
            loop[at : at + 1] = jnp.where(row == r, total, 0.0)


def up_kernel(
    own, below, above, u1, source, sigma, cells, loop, weight_ref, offset_ref,
    solution_ref, loop_out,
    u2s, r2s, s2, f2, u3s, r3s, s3, f3, buf2a, buf2b, buf3a, buf3b,
    n2, nf2, ns2, nu2s, nb2, start, buf_a, buf_b, corr_ref, stage,
):
    count = u1.shape[0]
    R, J = u1.shape[-2:]
    N = loop.shape[1]
    row = lax.axis_index("row")
    blk = lax.axis_index("blk")
    sub = rows_of(R, J)

    for at in range(8 * count + 4):
        if at < 8 * count:
            kind, rest = divmod(at, 4 * count)
            v, ab = divmod(rest, 4)
            a, b = divmod(ab, 2)
            dst = (u2s, r2s)[kind].at[v, a, b]
        else:
            a, b = divmod(at - 8 * count, 2)
            dst = s2.at[a, b]
        dst[:R] = own[at]
        dst[R : 2 * R] = above[at]
        dst[2 * R :] = below[at]

    for a in range(2):
        for b in range(2):
            res = residual(u2s, r2s, 1.0 + s2[a, b], 0.25, a, b, 2, 3 * R)
            for v in range(count):
                f2[v, a, b] = 2.0 * r2s[v, a, b] - res[v]
    first_section(buf2a, u2s, r2s, s2, 0.25, 1.0 / SECTIONS2, 2)
    src, dst = buf2a, buf2b
    for k in range(1, SECTIONS2):
        section(dst, src, u2s, f2, s2, 0.25, 1.0 / (SECTIONS2 - k), 2, 3 * R)
        src, dst = dst, src
    u2, r2 = src, dst
    for a in range(2):
        for b in range(2):
            res = residual(u2, f2, 1.0 + s2[a, b], 0.25, a, b, 2, 3 * R)
            for v in range(count):
                r2[v, a, b] = res[v]
    for v in range(count):
        u3s[v, 0, 0] = quarter(lambda i, j: u2[v, i, j])
        r3s[v, 0, 0] = quarter(lambda i, j: r2[v, i, j])
    s3[0, 0] = quarter(lambda i, j: s2[i, j])

    res = residual(u3s, r3s, 0.25 + s3[0, 0], 0.0625, 0, 0, 1, 3 * R)
    for v in range(count):
        f3[v, 0, 0] = 2.0 * r3s[v, 0, 0] - res[v]
    first_section(buf3a, u3s, r3s, s3, 0.0625, 1.0 / SECTIONS3, 1)
    src3, dst3 = buf3a, buf3b
    for k in range(1, SECTIONS3):
        section(dst3, src3, u3s, f3, s3, 0.0625, 1.0 / (SECTIONS3 - k), 1, 3 * R)
        src3, dst3 = dst3, src3

    def narrow(x):
        return x[:R], jnp.where(sub < R // 2, x[R : 2 * R], x[2 * R :])

    for v in range(count):
        gain = narrow(src3[v, 0, 0] - u3s[v, 0, 0])
        for a in range(2):
            for b in range(2):
                for part in range(2):
                    at = slice(part * R, (part + 1) * R)
                    n2[v, a, b, at] = narrow(u2[v, a, b])[part] + gain[part]
                    nf2[v, a, b, at] = narrow(f2[v, a, b])[part]
                    if v == 0:
                        ns2[a, b, at] = narrow(s2[a, b])[part]
    src, other = n2, nb2
    spare = nu2s
    for k in range(SECTIONS2):
        dst = (nb2, spare)[k % 2]
        section(dst, src, n2, nf2, ns2, 0.25, 1.0 / (SECTIONS2 - k), 2, 2 * R)
        src = dst

    half = loop.shape[0] // 2
    mine = jnp.where(row == 0, loop[:half], loop[half:])
    others = jnp.where(row == 0, loop[half:], loop[:half])
    offset = offset_ref[0]
    shift = lax.rem(jnp.where(row == 0, N - offset, offset), N)
    correction = weight_ref[...] * (mine + pltpu.roll(others, shift, 1))
    corr_ref[...] = correction
    length = loop_out.shape[2]
    away = lax.rem(N - blk * length, N)
    loop_out[0] = pltpu.roll(correction, away, 1)[:count, :length]

    for v in range(count):
        for a in range(FOLD):
            for b in range(FOLD):
                after = src[v, a // 2, b // 2]
                x = u2s[v, a // 2, b // 2]
                gain = (after[:R] - x[:R], after[R:] - narrow(x)[1])
                at = (v * FOLD + a) * FOLD + b
                k = (2 * count + 1) * 4 + at // R
                high = above[k, at % R : at % R + 1]
                low = below[k, at % R : at % R + 1]
                start[v, a, b, :R] = u1[v, a, b] + gain[0]
                start[v, a, b, R:] = jnp.where(sub < R // 2, high, low) + gain[1]
    lane = lanes_of(2 * R, J)
    ring = lanes_of(2 * R, N)
    last = jnp.logical_and(lane == J - 1, row == 0)
    first = jnp.logical_and(lane == 0, row == 1)
    for a in range(FOLD):
        match = cells[a, :, :1] == ring
        for v in range(count):
            fix = jnp.where(match, corr_ref[v : v + 1], 0.0)
            fix = jnp.sum(fix, axis=1, keepdims=True)
            start[v, a, FOLD - 1] = start[v, a, FOLD - 1] + jnp.where(last, fix, 0.0)
            start[v, a, 0] = start[v, a, 0] + jnp.where(first, fix, 0.0)
    src = start
    for k in range(SECTIONS1):
        dst = (buf_a, buf_b)[k % 2]
        rows = R if k == SECTIONS1 - 1 else 2 * R
        section(dst, src, start, source, sigma, 1.0, 1.0 / (SECTIONS1 - k), FOLD, rows)
        src = dst
    for v in range(count):
        for a in range(FOLD):
            for b in range(FOLD):
                stage[v, b, pl.ds(a, R, stride=FOLD), :] = src[v, a, b, :R]
        for c, x in enumerate(join_lanes([stage[v, b] for b in range(FOLD)])):
            solution_ref[0, v, :, c * J : (c + 1) * J] = x


def body(state, forcing, sigma, partner, loop_weight, offset):
    _, count, rows, cols = state.shape
    R, J = rows // FOLD, cols // FOLD
    N = loop_weight.shape[1]
    blocks = lax.axis_size("blk")
    length = N // blocks
    real = functools.partial(jax.ShapeDtypeStruct, dtype=jnp.float32)
    scratch = lambda *shape: pltpu.VMEM(shape, jnp.float32)
    deep = 2 * FOLD
    last = rows // deep - 1

    def ends(lead):
        zero = (0,) * len(lead)
        return [
            pl.BlockSpec(lead + (deep, cols), lambda i: zero + (0, 0)),
            pl.BlockSpec(lead + (deep, cols), lambda i: zero + (last, 0)),
        ]

    packed = real(((2 * count + 2) * FOLD, cols))
    whole = pl.BlockSpec(packed.shape, lambda i: (0, 0))
    head, tail = pl.pallas_call(
        pack_kernel,
        grid=(1,),
        in_specs=ends((1, count)) * 2 + ends((1,)) + [pl.BlockSpec((1, rows, 1), lambda i: (0, 0, 0))],
        out_specs=[whole, whole],
        out_shape=[packed, packed],
        name="pack",
    )(state, state, forcing, forcing, sigma, sigma, partner)
    up = [(i, (i + 1) % blocks) for i in range(blocks)]
    down = [((i + 1) % blocks, i) for i in range(blocks)]
    below = lax.ppermute(tail, "blk", up)
    above = lax.ppermute(head, "blk", down)

    st, fo, sg = pl.pallas_call(
        fold_kernel,
        in_specs=[vmem()] * 3,
        out_specs=[vmem()] * 3,
        out_shape=[
            real((count, FOLD, FOLD, R, J)),
            real((count, FOLD, FOLD, R, J)),
            real((FOLD, FOLD, R, J)),
        ],
        scratch_shapes=[scratch(2 * count + 1, FOLD, rows, J)],
        name="fold",
    )(state, forcing, sigma)

    tiles = (2 * count + 1) * 4
    message = real((tiles + count * FOLD * FOLD // R, R, J))
    fine = (count, FOLD, FOLD, 2 * R, J)
    u1, source, sigma_w, cells, head, tail, loop = pl.pallas_call(
        down_kernel,
        in_specs=[vmem()] * 6,
        out_specs=[vmem()] * 7,
        out_shape=[
            real((count, FOLD, FOLD, R, J)),
            real(fine),
            real((FOLD, FOLD, 2 * R, J)),
            jax.ShapeDtypeStruct((FOLD, 2 * R, J), jnp.int32),
            message,
            message,
            real((16, N)),
        ],
        scratch_shapes=[
            scratch(*fine),
            scratch(*fine),
            scratch(*fine),
            scratch(2 * count + 1, FOLD, 2 * FOLD, J),
            scratch(count, FOLD, FOLD, R, J),
            pltpu.VMEM((rows, J), jnp.int32),
        ],
        name="down",
    )(st, fo, sg, below, above, partner)

    below = lax.ppermute(tail, "blk", up)
    above = lax.ppermute(head, "blk", down)
    loop = loop + lax.ppermute(loop, "row", [(0, 1), (1, 0)])
    reach = 1
    while reach < blocks:
        loop = loop + lax.ppermute(loop, "blk", [(i, i ^ reach) for i in range(blocks)])
        reach *= 2

    mid = (count, 2, 2, 3 * R, J)
    low = (count, 1, 1, 3 * R, J)
    thin = (count, 2, 2, 2 * R, J)
    result, loop_out = pl.pallas_call(
        up_kernel,
        in_specs=[vmem()] * 9 + [pl.BlockSpec(memory_space=pltpu.SMEM)],
        out_specs=[vmem()] * 2,
        out_shape=[real(state.shape), real((1, count, length))],
        scratch_shapes=[
            scratch(*mid), scratch(*mid), scratch(*mid[1:]), scratch(*mid),
            scratch(*low), scratch(*low), scratch(*low[1:]), scratch(*low),
            scratch(*mid), scratch(*mid), scratch(*low), scratch(*low),
            scratch(*thin), scratch(*thin), scratch(*thin[1:]), scratch(*thin), scratch(*thin),
            scratch(*fine), scratch(*fine), scratch(*fine),
            scratch(8, N),
            scratch(count, FOLD, rows, J),
        ],
        name="up",
    )(head, below, above, u1, source, sigma_w, cells, loop, loop_weight, offset)
    return result, loop_out


def solution(mesh):
    placed = (
        P("row", None, "blk", None),
        P("row", None, "blk", None),
        P("row", "blk", None),
        P("row", "blk", None),
        P("row", None),
        P(),
    )
    return jax.shard_map(
        body,
        mesh=mesh,
        in_specs=placed,
        out_specs=(P("row", None, "blk", None), P("row", None, "blk")),
        check_vma=False,
    )
```

```python
import functools

import jax
import jax.numpy as jnp
from jax import lax
from jax.experimental import pallas as pl
from jax.experimental.pallas import tpu as pltpu
from jax.sharding import PartitionSpec as P


SECTIONS1 = 3
SECTIONS2 = 3
SECTIONS3 = 4
COEFF = 0.8

FOLD = 4
LIMIT = 24 * 1024 * 1024


def vmem():
    return pl.BlockSpec(memory_space=pltpu.VMEM)


def lanes_of(rows, cols):
    return lax.broadcasted_iota(jnp.int32, (rows, cols), 1)


def rows_of(rows, cols):
    return lax.broadcasted_iota(jnp.int32, (rows, cols), 0)


def pick(x, index):
    return jnp.take_along_axis(x, index, axis=1, mode="promise_in_bounds")


def split_lanes(x):
    rows, cols = x.shape
    wide = cols // FOLD
    run = wide // FOLD
    lane = lanes_of(rows, wide)
    parts = [x[:, c * wide : (c + 1) * wide] for c in range(FOLD)]
    group = lane // run
    out = []
    for b in range(FOLD):
        index = (lane % run) * FOLD + b
        taken = [pick(p, index) for p in parts]
        value = taken[-1]
        for c in range(FOLD - 1):
            value = jnp.where(group == c, taken[c], value)
        out.append(value)
    return out


def join_lanes(parts):
    rows, wide = parts[0].shape
    run = wide // FOLD
    lane = lanes_of(rows, wide)
    turn = lane % FOLD
    out = []
    for c in range(FOLD):
        index = lane // FOLD + c * run
        taken = [pick(p, index) for p in parts]
        value = taken[-1]
        for b in range(FOLD - 1):
            value = jnp.where(turn == b, taken[b], value)
        out.append(value)
    return out


def residual(src, source, diag, scale, a, b, fold, rows):
    count = src.shape[0]
    total, wide = src.shape[-2:]
    u = [src[v, a, b][:rows] for v in range(count)]
    q = u[0] * u[0]
    for v in range(1, count):
        q = q + u[v] * u[v]
    q = q * (1.0 / count)
    factor = diag + 0.5 * q / (1.0 + q)
    lane = lanes_of(rows, wide)
    out = []
    for v in range(count):
        up = src[v, a - 1, b] if a else pltpu.roll(src[v, fold - 1, b], 1, 0)
        down = src[v, a + 1, b] if a < fold - 1 else pltpu.roll(src[v, 0, b], total - 1, 0)
        if b:
            left = src[v, a, b - 1][:rows]
        else:
            left = jnp.where(lane == 0, 0.0, pltpu.roll(src[v, a, fold - 1][:rows], 1, 1))
        if b < fold - 1:
            right = src[v, a, b + 1][:rows]
        else:
            right = jnp.where(lane == wide - 1, 0.0, pltpu.roll(src[v, a, 0][:rows], wide - 1, 1))
        near = (up[:rows] + down[:rows]) + (left + right)
        out.append(source[v, a, b][:rows] + scale * near - factor * u[v])
    return out


def section(dst, src, start, source, sigma, scale, weight, fold, rows):
    for a in range(fold):
        for b in range(fold):
            diag = 4.0 * scale + sigma[a, b][:rows]
            step = weight * (COEFF / (diag + 1.5))
            res = residual(src, source, diag, scale, a, b, fold, rows)
            for v, r in enumerate(res):
                dst[v, a, b, :rows] = start[v, a, b][:rows] + step * r


def first_section(dst, start, coarse, sigma, scale, weight, fold):
    for a in range(fold):
        for b in range(fold):
            step = weight * (COEFF / (4.0 * scale + sigma[a, b] + 1.5))
            for v in range(dst.shape[0]):
                dst[v, a, b] = start[v, a, b] + step * coarse[v, a, b]


def quarter(x):
    return 0.25 * ((x(0, 0) + x(0, 1)) + (x(1, 0) + x(1, 1)))


def wrap(x, size):
    return x & (size - 1) if size & (size - 1) == 0 else lax.rem(x, size)


def fetch(pairs, sems):
    copies = [pltpu.make_async_copy(x, y, sems.at[k]) for k, (x, y) in enumerate(pairs)]
    for copy in copies:
        copy.start()
    for copy in copies:
        copy.wait()


def pack_kernel(s_ref, f_ref, g_ref, p_ref, head, tail, s_end, f_end, g_end, slots, sems):
    count, rows = s_ref.shape[1:3]
    edge = FOLD
    deep = 2 * edge
    parts = (slice(0, deep), slice(rows - deep, rows))
    pairs = [(p_ref, slots)]
    for k, part in enumerate(parts):
        pairs += [
            (s_ref.at[0, :, part], s_end.at[k]),
            (f_ref.at[0, :, part], f_end.at[k]),
            (g_ref.at[0, part], g_end.at[k]),
        ]
    fetch(pairs, sems)
    for k, message in enumerate((head, tail)):
        keep = slice(0, edge) if k == 0 else slice(deep - edge, deep)
        for v in range(count):
            message[v * edge : (v + 1) * edge] = s_end[k, v, keep]
            message[(count + v) * edge : (count + v + 1) * edge] = f_end[k, v, keep]
        at = 2 * count * edge
        message[at : at + edge] = g_end[k, keep]
        at += edge
        message[at : at + edge] = jnp.zeros((edge, message.shape[1]), jnp.float32)
        message[at : at + 1, :rows] = slots[...].astype(jnp.float32)


def fold_kernel(
    s_hbm, f_hbm, g_hbm, p_hbm, st, fo, sg, own_slot,
    s_ref, f_ref, g_ref, p_ref, stage, slots, sems,
):
    count = st.shape[0]
    R, _ = st.shape[-2:]
    rows = s_hbm.shape[2]
    fetch(((s_hbm.at[0], s_ref), (f_hbm.at[0], f_ref), (g_hbm.at[0], g_ref), (p_hbm, p_ref)), sems)
    for ch in range(2 * count + 1):
        kind, v = divmod(ch, count)
        x = g_ref[...] if kind == 2 else (s_ref, f_ref)[kind][v]
        for b, part in enumerate(split_lanes(x)):
            stage[ch, b] = part
        for a in range(FOLD):
            for b in range(FOLD):
                part = stage[ch, b, pl.ds(a, R, stride=FOLD), :]
                if kind == 2:
                    sg[a, b] = part
                else:
                    (st, fo)[kind][v, a, b] = part
    diagonal = lanes_of(rows, rows) == rows_of(rows, rows)
    column = jnp.where(diagonal, p_ref[...].astype(jnp.float32), 0.0)
    column = jnp.sum(column, axis=1, keepdims=True).astype(jnp.int32)
    slots[...] = jnp.broadcast_to(column, slots.shape)
    for a in range(FOLD):
        own_slot[a] = slots[pl.ds(a, R, stride=FOLD), :]


def down_kernel(
    st, fo, sg, own_slot, below, above,
    u1, source, sigma, cells, head, tail, loop,
    start, buf_a, buf_b, edge_buf, resid, own_loop,
):
    count = st.shape[0]
    R, J = st.shape[-2:]
    N = loop.shape[2]
    edge = FOLD
    row = lax.axis_index("row")
    blk = lax.axis_index("blk")
    blocks = lax.axis_size("blk")
    sub = rows_of(R, J)
    for ch in range(2 * count + 1):
        x = jnp.concatenate(
            [below[ch * edge : (ch + 1) * edge], above[ch * edge : (ch + 1) * edge]], axis=0
        )
        for b, part in enumerate(split_lanes(x)):
            edge_buf[ch, b] = part

    def halo(ch, a, b):
        low = edge_buf[ch, b, a : a + 1]
        high = edge_buf[ch, b, edge + a : edge + a + 1]
        return jnp.where(sub == 0, high, jnp.where(sub == R - 1, low, 0.0))

    rows = R * FOLD
    at = (2 * count + 1) * edge
    place = lanes_of(1, rows)

    def slot_of(message, i):
        x = jnp.where(place == i, message[at : at + 1, :rows], 0.0)
        return jnp.sum(x, axis=1, keepdims=True).astype(jnp.int32)

    for a in range(FOLD):
        for b in range(FOLD):
            for v in range(count):
                start[v, a, b, :R] = st[v, a, b]
                start[v, a, b, R:] = halo(v, a, b)
                source[v, a, b, :R] = fo[v, a, b]
                source[v, a, b, R:] = halo(count + v, a, b)
            sigma[a, b, :R] = sg[a, b]
            sigma[a, b, R:] = halo(2 * count, a, b)
        own = own_slot[a]
        low = jnp.broadcast_to(slot_of(below, rows - edge + a), (R, J))
        high = jnp.broadcast_to(slot_of(above, a), (R, J))
        cells[a, :R] = wrap(own * blocks + blk, N)
        cells[a, R:] = jnp.where(
            sub < R // 2,
            wrap(high * blocks + lax.rem(blk + 1, blocks), N),
            wrap(low * blocks + lax.rem(blk + blocks - 1, blocks), N),
        )

    src = start
    for k in range(SECTIONS1):
        dst = (buf_a, buf_b)[k % 2]
        section(dst, src, start, source, sigma, 1.0, 1.0 / (SECTIONS1 - k), FOLD, 2 * R)
        src = dst

    for a in range(FOLD):
        for b in range(FOLD):
            res = residual(src, source, 4.0 + sigma[a, b][:R], 1.0, a, b, FOLD, R)
            for v in range(count):
                resid[v, a, b] = res[v]
                u = src[v, a, b][:R]
                u1[v, a, b] = u
                at = (v * FOLD + a) * FOLD + b
                k = (2 * count + 1) * 4 + at // R
                head[k, at % R : at % R + 1] = u[:1]
                tail[k, at % R : at % R + 1] = u[R - 1 :]
    for a in range(2):
        for b in range(2):
            for v in range(count):
                at = (v * 2 + a) * 2 + b
                x = quarter(lambda i, j: u1[v, 2 * a + i, 2 * b + j])
                head[at] = x
                tail[at] = x
                at += 4 * count
                x = quarter(lambda i, j: resid[v, 2 * a + i, 2 * b + j])
                head[at] = x
                tail[at] = x
            at = 8 * count + a * 2 + b
            x = quarter(lambda i, j: sg[2 * a + i, 2 * b + j])
            head[at] = x
            tail[at] = x

    lane = lanes_of(R, J)
    ring = lanes_of(R, N)
    sums = [jnp.zeros((R, N), jnp.float32) for _ in range(count)]
    column = jnp.where(row == 0, J - 1, 0)
    for a in range(FOLD):
        match = cells[a, :R, :1] == ring
        for v in range(count):
            face = jnp.where(row == 0, resid[v, a, FOLD - 1], resid[v, a, 0])
            face = jnp.sum(jnp.where(lane == column, face, 0.0), axis=1, keepdims=True)
            sums[v] = sums[v] + jnp.where(match, face, 0.0)
    own_loop[...] = jnp.zeros_like(own_loop)
    for v in range(count):
        own_loop[v : v + 1] = jnp.sum(sums[v], axis=0, keepdims=True)
    loop[...] = jnp.broadcast_to(own_loop[...][None], loop.shape)


def up_kernel(
    own, below, above, u1, source, sigma, cells, loop, weight_hbm, offset_ref,
    solution_ref, loop_out,
    u2s, r2s, s2, f2, u3s, r3s, s3, f3, buf2a, buf2b, buf3a, buf3b,
    n2, nf2, ns2, nu2s, nb2, start, buf_a, buf_b, corr_ref, stage, weight_ref, sem,
):
    count = u1.shape[0]
    R, J = u1.shape[-2:]
    N = loop.shape[2]
    row = lax.axis_index("row")
    blk = lax.axis_index("blk")
    sub = rows_of(R, J)
    weights = pltpu.make_async_copy(weight_hbm, weight_ref, sem)
    weights.start()

    for at in range(8 * count + 4):
        if at < 8 * count:
            kind, rest = divmod(at, 4 * count)
            v, ab = divmod(rest, 4)
            a, b = divmod(ab, 2)
            dst = (u2s, r2s)[kind].at[v, a, b]
        else:
            a, b = divmod(at - 8 * count, 2)
            dst = s2.at[a, b]
        dst[:R] = own[at]
        dst[R : 2 * R] = above[at]
        dst[2 * R :] = below[at]

    for a in range(2):
        for b in range(2):
            res = residual(u2s, r2s, 1.0 + s2[a, b], 0.25, a, b, 2, 3 * R)
            for v in range(count):
                f2[v, a, b] = 2.0 * r2s[v, a, b] - res[v]
    first_section(buf2a, u2s, r2s, s2, 0.25, 1.0 / SECTIONS2, 2)
    src, dst = buf2a, buf2b
    for k in range(1, SECTIONS2):
        section(dst, src, u2s, f2, s2, 0.25, 1.0 / (SECTIONS2 - k), 2, 3 * R)
        src, dst = dst, src
    u2, r2 = src, dst
    for a in range(2):
        for b in range(2):
            res = residual(u2, f2, 1.0 + s2[a, b], 0.25, a, b, 2, 3 * R)
            for v in range(count):
                r2[v, a, b] = res[v]
    for v in range(count):
        u3s[v, 0, 0] = quarter(lambda i, j: u2[v, i, j])
        r3s[v, 0, 0] = quarter(lambda i, j: r2[v, i, j])
    s3[0, 0] = quarter(lambda i, j: s2[i, j])

    res = residual(u3s, r3s, 0.25 + s3[0, 0], 0.0625, 0, 0, 1, 3 * R)
    for v in range(count):
        f3[v, 0, 0] = 2.0 * r3s[v, 0, 0] - res[v]
    first_section(buf3a, u3s, r3s, s3, 0.0625, 1.0 / SECTIONS3, 1)
    src3, dst3 = buf3a, buf3b
    for k in range(1, SECTIONS3):
        section(dst3, src3, u3s, f3, s3, 0.0625, 1.0 / (SECTIONS3 - k), 1, 3 * R)
        src3, dst3 = dst3, src3

    def narrow(x):
        return x[:R], jnp.where(sub < R // 2, x[R : 2 * R], x[2 * R :])

    for v in range(count):
        gain = narrow(src3[v, 0, 0] - u3s[v, 0, 0])
        for a in range(2):
            for b in range(2):
                for part in range(2):
                    at = slice(part * R, (part + 1) * R)
                    n2[v, a, b, at] = narrow(u2[v, a, b])[part] + gain[part]
                    nf2[v, a, b, at] = narrow(f2[v, a, b])[part]
                    if v == 0:
                        ns2[a, b, at] = narrow(s2[a, b])[part]
    src = n2
    spare = nu2s
    for k in range(SECTIONS2):
        dst = (nb2, spare)[k % 2]
        section(dst, src, n2, nf2, ns2, 0.25, 1.0 / (SECTIONS2 - k), 2, 2 * R)
        src = dst

    half = loop.shape[0] // 2
    rotor = jnp.sum(loop[:half], axis=0)
    stator = jnp.sum(loop[half:], axis=0)
    mine = jnp.where(row == 0, rotor, stator)
    others = jnp.where(row == 0, stator, rotor)
    offset = offset_ref[0]
    weights.wait()
    shift = lax.rem(jnp.where(row == 0, N - offset, offset), N)
    correction = weight_ref[...] * (mine + pltpu.roll(others, shift, 1))
    corr_ref[...] = correction
    length = loop_out.shape[2]
    away = lax.rem(N - blk * length, N)
    shown = pltpu.roll(correction, away, 1)
    for v in range(count):
        loop_out[v] = shown[v : v + 1, :length]

    for v in range(count):
        for a in range(FOLD):
            for b in range(FOLD):
                after = src[v, a // 2, b // 2]
                x = u2s[v, a // 2, b // 2]
                gain = (after[:R] - x[:R], after[R:] - narrow(x)[1])
                at = (v * FOLD + a) * FOLD + b
                k = (2 * count + 1) * 4 + at // R
                high = above[k, at % R : at % R + 1]
                low = below[k, at % R : at % R + 1]
                start[v, a, b, :R] = u1[v, a, b] + gain[0]
                start[v, a, b, R:] = jnp.where(sub < R // 2, high, low) + gain[1]
    lane = lanes_of(2 * R, J)
    ring = lanes_of(2 * R, N)
    last = jnp.logical_and(lane == J - 1, row == 0)
    first = jnp.logical_and(lane == 0, row == 1)
    for a in range(FOLD):
        match = cells[a, :, :1] == ring
        for v in range(count):
            fix = jnp.where(match, corr_ref[v : v + 1], 0.0)
            fix = jnp.sum(fix, axis=1, keepdims=True)
            start[v, a, FOLD - 1] = start[v, a, FOLD - 1] + jnp.where(last, fix, 0.0)
            start[v, a, 0] = start[v, a, 0] + jnp.where(first, fix, 0.0)
    src = start
    for k in range(SECTIONS1):
        dst = (buf_a, buf_b)[k % 2]
        rows = R if k == SECTIONS1 - 1 else 2 * R
        section(dst, src, start, source, sigma, 1.0, 1.0 / (SECTIONS1 - k), FOLD, rows)
        src = dst
    for v in range(count):
        for a in range(FOLD):
            for b in range(FOLD):
                stage[v, b, pl.ds(a, R, stride=FOLD), :] = src[v, a, b, :R]
        for c, x in enumerate(join_lanes([stage[v, b] for b in range(FOLD)])):
            solution_ref[0, v, :, c * J : (c + 1) * J] = x


def body(state, forcing, sigma, partner, loop_weight, offset):
    _, count, rows, cols = state.shape
    R, J = rows // FOLD, cols // FOLD
    N = loop_weight.shape[1]
    blocks = lax.axis_size("blk")
    length = N // blocks
    real = functools.partial(jax.ShapeDtypeStruct, dtype=jnp.float32)
    near = lambda shape, dtype=jnp.float32: pltpu.VMEM(shape, dtype)
    away = lambda x: pltpu.with_memory_space_constraint(x, pltpu.HBM)
    held = lambda x: pltpu.with_memory_space_constraint(x, pltpu.VMEM)
    scratch = lambda *shape: pltpu.VMEM(shape, jnp.float32)
    far = pl.BlockSpec(memory_space=pltpu.HBM)
    deep = 2 * FOLD
    slots = partner[:, :, 0]
    packed = near(((2 * count + 2) * FOLD, cols))
    limit = pltpu.CompilerParams(vmem_limit_bytes=LIMIT)
    head, tail = pl.pallas_call(
        pack_kernel,
        in_specs=[far] * 4,
        out_specs=[vmem()] * 2,
        out_shape=[packed, packed],
        scratch_shapes=[
            scratch(2, count, deep, cols),
            scratch(2, count, deep, cols),
            scratch(2, deep, cols),
            pltpu.VMEM((1, rows), jnp.int32),
            pltpu.SemaphoreType.DMA((7,)),
        ],
        compiler_params=limit,
        name="pack",
    )(away(state), away(forcing), away(sigma), away(slots))
    up = [(i, (i + 1) % blocks) for i in range(blocks)]
    down = [((i + 1) % blocks, i) for i in range(blocks)]
    below = lax.ppermute(tail, "blk", up)
    above = lax.ppermute(head, "blk", down)

    st, fo, sg, own_slot = pl.pallas_call(
        fold_kernel,
        in_specs=[far] * 4,
        out_specs=[vmem()] * 4,
        out_shape=[
            near((count, FOLD, FOLD, R, J)),
            near((count, FOLD, FOLD, R, J)),
            near((FOLD, FOLD, R, J)),
            near((FOLD, R, J), jnp.int32),
        ],
        scratch_shapes=[
            scratch(count, rows, cols),
            scratch(count, rows, cols),
            scratch(rows, cols),
            pltpu.VMEM((1, rows), jnp.int32),
            scratch(2 * count + 1, FOLD, rows, J),
            pltpu.VMEM((rows, J), jnp.int32),
            pltpu.SemaphoreType.DMA((4,)),
        ],
        compiler_params=limit,
        name="fold",
    )(away(state), away(forcing), away(sigma), away(slots))

    tiles = (2 * count + 1) * 4
    message = near((tiles + count * FOLD * FOLD // R, R, J))
    fine = (count, FOLD, FOLD, 2 * R, J)
    u1, source, sigma_w, cells, head, tail, loop = pl.pallas_call(
        down_kernel,
        in_specs=[vmem()] * 6,
        out_specs=[vmem()] * 7,
        out_shape=[
            near((count, FOLD, FOLD, R, J)),
            near(fine),
            near((FOLD, FOLD, 2 * R, J)),
            near((FOLD, 2 * R, J), jnp.int32),
            message,
            message,
            near((2 * blocks, 8, N)),
        ],
        scratch_shapes=[
            scratch(*fine),
            scratch(*fine),
            scratch(*fine),
            scratch(2 * count + 1, FOLD, 2 * FOLD, J),
            scratch(count, FOLD, FOLD, R, J),
            scratch(8, N),
        ],
        compiler_params=limit,
        name="down",
    )(held(st), held(fo), held(sg), held(own_slot), held(below), held(above))

    below = lax.ppermute(tail, "blk", up)
    above = lax.ppermute(head, "blk", down)
    loop = lax.all_to_all(loop, ("row", "blk"), 0, 0, tiled=True)

    mid = (count, 2, 2, 3 * R, J)
    low = (count, 1, 1, 3 * R, J)
    thin = (count, 2, 2, 2 * R, J)
    result, loop_out = pl.pallas_call(
        up_kernel,
        in_specs=[vmem()] * 8 + [far, pl.BlockSpec(memory_space=pltpu.SMEM)],
        out_specs=[vmem()] * 2,
        out_shape=[real(state.shape), real((count, 1, length))],
        scratch_shapes=[
            scratch(*mid), scratch(*mid), scratch(*mid[1:]), scratch(*mid),
            scratch(*low), scratch(*low), scratch(*low[1:]), scratch(*low),
            scratch(*mid), scratch(*mid), scratch(*low), scratch(*low),
            scratch(*thin), scratch(*thin), scratch(*thin[1:]), scratch(*thin), scratch(*thin),
            scratch(*fine), scratch(*fine), scratch(*fine),
            scratch(8, N),
            scratch(count, FOLD, rows, J),
            scratch(1, N),
            pltpu.SemaphoreType.DMA(()),
        ],
        compiler_params=limit,
        name="up",
    )(
        held(head), held(below), held(above), held(u1), held(source), held(sigma_w), held(cells),
        held(loop), away(loop_weight), offset,
    )
    return result, jnp.transpose(loop_out, (1, 0, 2))


def solution(mesh):
    placed = (
        P("row", None, "blk", None),
        P("row", None, "blk", None),
        P("row", "blk", None),
        P("row", "blk", None),
        P("row", None),
        P(),
    )

    return jax.shard_map(
        body,
        mesh=mesh,
        in_specs=placed,
        out_specs=(P("row", None, "blk", None), P("row", None, "blk")),
        check_vma=False,
    )
```

```python
import functools

import jax
import jax.numpy as jnp
from jax import lax
from jax.experimental import pallas as pl
from jax.experimental.pallas import tpu as pltpu
from jax.sharding import PartitionSpec as P


SECTIONS1 = 3
SECTIONS2 = 3
SECTIONS3 = 4
COEFF = 0.8

FOLD = 4
LIMIT = 24 * 1024 * 1024


def vmem():
    return pl.BlockSpec(memory_space=pltpu.VMEM)


def lanes_of(rows, cols):
    return lax.broadcasted_iota(jnp.int32, (rows, cols), 1)


def rows_of(rows, cols):
    return lax.broadcasted_iota(jnp.int32, (rows, cols), 0)


def pick(x, index):
    return jnp.take_along_axis(x, index, axis=1, mode="promise_in_bounds")


def split_lanes(x):
    rows, cols = x.shape
    wide = cols // FOLD
    run = wide // FOLD
    lane = lanes_of(rows, wide)
    parts = [x[:, c * wide : (c + 1) * wide] for c in range(FOLD)]
    group = lane // run
    out = []
    for b in range(FOLD):
        index = (lane % run) * FOLD + b
        taken = [pick(p, index) for p in parts]
        value = taken[-1]
        for c in range(FOLD - 1):
            value = jnp.where(group == c, taken[c], value)
        out.append(value)
    return out


def join_lanes(parts):
    rows, wide = parts[0].shape
    run = wide // FOLD
    lane = lanes_of(rows, wide)
    turn = lane % FOLD
    out = []
    for c in range(FOLD):
        index = lane // FOLD + c * run
        taken = [pick(p, index) for p in parts]
        value = taken[-1]
        for b in range(FOLD - 1):
            value = jnp.where(turn == b, taken[b], value)
        out.append(value)
    return out


def residual(src, source, diag, scale, a, b, fold, rows):
    count = src.shape[0]
    total, wide = src.shape[-2:]
    u = [src[v, a, b][:rows] for v in range(count)]
    q = u[0] * u[0]
    for v in range(1, count):
        q = q + u[v] * u[v]
    q = q * (1.0 / count)
    factor = diag + 0.5 * q / (1.0 + q)
    lane = lanes_of(rows, wide)
    out = []
    for v in range(count):
        up = src[v, a - 1, b] if a else pltpu.roll(src[v, fold - 1, b], 1, 0)
        down = src[v, a + 1, b] if a < fold - 1 else pltpu.roll(src[v, 0, b], total - 1, 0)
        if b:
            left = src[v, a, b - 1][:rows]
        else:
            left = jnp.where(lane == 0, 0.0, pltpu.roll(src[v, a, fold - 1][:rows], 1, 1))
        if b < fold - 1:
            right = src[v, a, b + 1][:rows]
        else:
            right = jnp.where(lane == wide - 1, 0.0, pltpu.roll(src[v, a, 0][:rows], wide - 1, 1))
        near = (up[:rows] + down[:rows]) + (left + right)
        out.append(source[v, a, b][:rows] + scale * near - factor * u[v])
    return out


def section(dst, src, start, source, sigma, scale, weight, fold, rows):
    for a in range(fold):
        for b in range(fold):
            diag = 4.0 * scale + sigma[a, b][:rows]
            step = weight * (COEFF / (diag + 1.5))
            res = residual(src, source, diag, scale, a, b, fold, rows)
            for v, r in enumerate(res):
                dst[v, a, b, :rows] = start[v, a, b][:rows] + step * r


def first_section(dst, start, coarse, sigma, scale, weight, fold):
    for a in range(fold):
        for b in range(fold):
            step = weight * (COEFF / (4.0 * scale + sigma[a, b] + 1.5))
            for v in range(dst.shape[0]):
                dst[v, a, b] = start[v, a, b] + step * coarse[v, a, b]


def quarter(x):
    return 0.25 * ((x(0, 0) + x(0, 1)) + (x(1, 0) + x(1, 1)))


def wrap(x, size):
    return x & (size - 1) if size & (size - 1) == 0 else lax.rem(x, size)


def fetch(pairs, sems):
    copies = [pltpu.make_async_copy(x, y, sems.at[k]) for k, (x, y) in enumerate(pairs)]
    for copy in copies:
        copy.start()
    for copy in copies:
        copy.wait()


def edge_rows(count):
    out = []
    at = 0
    for kind, width in ((0, SECTIONS1 + 1), (1, SECTIONS1), (2, SECTIONS1)):
        for v in range(1 if kind == 2 else count):
            out.append((kind, v, at, width))
            at += width
    return out, at


def pack_kernel(s_hbm, f_hbm, g_hbm, p_hbm, head, tail, s_ref, f_ref, g_ref, p_ref, sems):
    count, rows = s_ref.shape[:2]
    fetch(((p_hbm, p_ref), (s_hbm.at[0], s_ref), (f_hbm.at[0], f_ref), (g_hbm.at[0], g_ref)), sems)
    places, end = edge_rows(count)
    for kind, v, at, width in places:
        x = g_ref if kind == 2 else (s_ref, f_ref)[kind].at[v]
        head[at : at + width] = x[:width]
        tail[at : at + width] = x[rows - width :]
    for message in (head, tail):
        message[end:] = jnp.zeros((message.shape[0] - end, message.shape[1]), jnp.float32)
        message[end : end + 1, :rows] = p_ref[...].astype(jnp.float32)


def fold_kernel(s_ref, f_ref, g_ref, p_ref, st, fo, sg, own_slot, stage, slots):
    count = st.shape[0]
    R, _ = st.shape[-2:]
    rows = s_ref.shape[1]
    for ch in range(2 * count + 1):
        kind, v = divmod(ch, count)
        x = g_ref[...] if kind == 2 else (s_ref, f_ref)[kind][v]
        for b, part in enumerate(split_lanes(x)):
            stage[ch, b] = part
        for a in range(FOLD):
            for b in range(FOLD):
                part = stage[ch, b, pl.ds(a, R, stride=FOLD), :]
                if kind == 2:
                    sg[a, b] = part
                else:
                    (st, fo)[kind][v, a, b] = part
    diagonal = lanes_of(rows, rows) == rows_of(rows, rows)
    column = jnp.where(diagonal, p_ref[...].astype(jnp.float32), 0.0)
    column = jnp.sum(column, axis=1, keepdims=True).astype(jnp.int32)
    slots[...] = jnp.broadcast_to(column, slots.shape)
    for a in range(FOLD):
        own_slot[a] = slots[pl.ds(a, R, stride=FOLD), :]


def down_kernel(
    st, fo, sg, own_slot, below, above,
    u1, source, sigma, cells, head, tail, loop,
    start, buf_a, buf_b, edge_buf, box, resid, own_loop,
):
    count = st.shape[0]
    R, J = st.shape[-2:]
    edge = FOLD
    row = lax.axis_index("row")
    blk = lax.axis_index("blk")
    blocks = lax.axis_size("blk")
    slots = own_loop.shape[1]
    N = blocks * slots
    sub = rows_of(R, J)
    places, end = edge_rows(count)
    for ch, (kind, v, at, width) in enumerate(places):
        if width < edge:
            box[...] = jnp.zeros_like(box)
        box[edge - width : edge] = below[at : at + width]
        box[edge : edge + width] = above[at : at + width]
        for b, part in enumerate(split_lanes(box[...])):
            edge_buf[ch, b] = part

    def halo(ch, a, b):
        low = edge_buf[ch, b, a : a + 1]
        high = edge_buf[ch, b, edge + a : edge + a + 1]
        return jnp.where(sub == 0, high, jnp.where(sub == R - 1, low, 0.0))

    rows = R * FOLD
    place = lanes_of(1, rows)

    def slot_of(message, i):
        x = jnp.where(place == i, message[end : end + 1, :rows], 0.0)
        return jnp.sum(x, axis=1, keepdims=True).astype(jnp.int32)

    for a in range(FOLD):
        for b in range(FOLD):
            for v in range(count):
                start[v, a, b, :R] = st[v, a, b]
                start[v, a, b, R:] = halo(v, a, b)
                source[v, a, b, :R] = fo[v, a, b]
                source[v, a, b, R:] = halo(count + v, a, b)
            sigma[a, b, :R] = sg[a, b]
            sigma[a, b, R:] = halo(2 * count, a, b)
        own = own_slot[a]
        low = jnp.broadcast_to(slot_of(below, rows - edge + a), (R, J))
        high = jnp.broadcast_to(slot_of(above, a), (R, J))
        cells[a, :R] = wrap(own * blocks + blk, N)
        cells[a, R:] = jnp.where(
            sub < R // 2,
            wrap(high * blocks + lax.rem(blk + 1, blocks), N),
            wrap(low * blocks + lax.rem(blk + blocks - 1, blocks), N),
        )

    src = start
    for k in range(SECTIONS1):
        dst = (buf_a, buf_b)[k % 2]
        section(dst, src, start, source, sigma, 1.0, 1.0 / (SECTIONS1 - k), FOLD, 2 * R)
        src = dst

    for a in range(FOLD):
        for b in range(FOLD):
            res = residual(src, source, 4.0 + sigma[a, b][:R], 1.0, a, b, FOLD, R)
            for v in range(count):
                resid[v, a, b] = res[v]
                u = src[v, a, b][:R]
                u1[v, a, b] = u
                at = (v * SECTIONS1 + a) * FOLD + b
                k = (2 * count + 1) * 4 + at // R
                if a < SECTIONS1:
                    head[k, at % R : at % R + 1] = u[:1]
                at -= FOLD * (FOLD - SECTIONS1)
                k = (2 * count + 1) * 4 + at // R
                if a >= FOLD - SECTIONS1:
                    tail[k, at % R : at % R + 1] = u[R - 1 :]
    for a in range(2):
        for b in range(2):
            for v in range(count):
                at = (v * 2 + a) * 2 + b
                x = quarter(lambda i, j: u1[v, 2 * a + i, 2 * b + j])
                head[at] = x
                tail[at] = x
                at += 4 * count
                x = quarter(lambda i, j: resid[v, 2 * a + i, 2 * b + j])
                head[at] = x
                tail[at] = x
            at = 8 * count + a * 2 + b
            x = quarter(lambda i, j: sg[2 * a + i, 2 * b + j])
            head[at] = x
            tail[at] = x

    lane = lanes_of(R, J)
    column = jnp.where(row == 0, J - 1, 0)
    sums = jnp.zeros((R, J), jnp.float32)
    for a in range(FOLD):
        slot = wrap(own_slot[a], slots)
        for v in range(count):
            face = jnp.where(row == 0, resid[v, a, FOLD - 1], resid[v, a, 0])
            face = jnp.sum(jnp.where(lane == column, face, 0.0), axis=1, keepdims=True)
            sums = sums + jnp.where(lane == slot + v * slots, face, 0.0)
    loop[...] = jnp.broadcast_to(jnp.sum(sums, axis=0, keepdims=True), loop.shape)


def up_kernel(
    own, below, above, u1, source, sigma, cells, loop, weight_hbm, offset_ref,
    solution_ref, loop_out,
    u2s, r2s, s2, f2, u3s, r3s, s3, f3, buf2a, buf2b, buf3a, buf3b,
    n2, nf2, ns2, nu2s, nb2, start, buf_a, buf_b, corr_ref, stage, weight_ref, sem,
):
    count = u1.shape[0]
    R, J = u1.shape[-2:]
    N = corr_ref.shape[1]
    row = lax.axis_index("row")
    blk = lax.axis_index("blk")
    blocks = lax.axis_size("blk")
    sub = rows_of(R, J)
    weights = pltpu.make_async_copy(weight_hbm, weight_ref, sem)
    weights.start()

    for at in range(8 * count + 4):
        if at < 8 * count:
            kind, rest = divmod(at, 4 * count)
            v, ab = divmod(rest, 4)
            a, b = divmod(ab, 2)
            dst = (u2s, r2s)[kind].at[v, a, b]
        else:
            a, b = divmod(at - 8 * count, 2)
            dst = s2.at[a, b]
        dst[:R] = own[at]
        dst[R : 2 * R] = above[at]
        dst[2 * R :] = below[at]

    for a in range(2):
        for b in range(2):
            res = residual(u2s, r2s, 1.0 + s2[a, b], 0.25, a, b, 2, 3 * R)
            for v in range(count):
                f2[v, a, b] = 2.0 * r2s[v, a, b] - res[v]
    first_section(buf2a, u2s, r2s, s2, 0.25, 1.0 / SECTIONS2, 2)
    src, dst = buf2a, buf2b
    for k in range(1, SECTIONS2):
        section(dst, src, u2s, f2, s2, 0.25, 1.0 / (SECTIONS2 - k), 2, 3 * R)
        src, dst = dst, src
    u2, r2 = src, dst
    for a in range(2):
        for b in range(2):
            res = residual(u2, f2, 1.0 + s2[a, b], 0.25, a, b, 2, 3 * R)
            for v in range(count):
                r2[v, a, b] = res[v]
    for v in range(count):
        u3s[v, 0, 0] = quarter(lambda i, j: u2[v, i, j])
        r3s[v, 0, 0] = quarter(lambda i, j: r2[v, i, j])
    s3[0, 0] = quarter(lambda i, j: s2[i, j])

    res = residual(u3s, r3s, 0.25 + s3[0, 0], 0.0625, 0, 0, 1, 3 * R)
    for v in range(count):
        f3[v, 0, 0] = 2.0 * r3s[v, 0, 0] - res[v]
    first_section(buf3a, u3s, r3s, s3, 0.0625, 1.0 / SECTIONS3, 1)
    src3, dst3 = buf3a, buf3b
    for k in range(1, SECTIONS3):
        section(dst3, src3, u3s, f3, s3, 0.0625, 1.0 / (SECTIONS3 - k), 1, 3 * R)
        src3, dst3 = dst3, src3

    def narrow(x):
        return x[:R], jnp.where(sub < R // 2, x[R : 2 * R], x[2 * R :])

    for v in range(count):
        gain = narrow(src3[v, 0, 0] - u3s[v, 0, 0])
        for a in range(2):
            for b in range(2):
                for part in range(2):
                    at = slice(part * R, (part + 1) * R)
                    n2[v, a, b, at] = narrow(u2[v, a, b])[part] + gain[part]
                    nf2[v, a, b, at] = narrow(f2[v, a, b])[part]
                    if v == 0:
                        ns2[a, b, at] = narrow(s2[a, b])[part]
    src = n2
    spare = nu2s
    for k in range(SECTIONS2):
        dst = (nb2, spare)[k % 2]
        section(dst, src, n2, nf2, ns2, 0.25, 1.0 / (SECTIONS2 - k), 2, 2 * R)
        src = dst

    slots = N // blocks
    wide = loop.shape[1]
    offset = offset_ref[0]
    shift = lax.rem(jnp.where(row == 0, N - offset, offset), N)
    weights.wait()
    both = []
    for r in range(2):
        held = loop[r * blocks : (r + 1) * blocks]
        for v in range(count):
            for c in range(0, N, wide):
                cell = lanes_of(blocks, wide) + c
                value = pick(held, cell // blocks + v * slots)
                value = jnp.where(wrap(cell, blocks) == rows_of(blocks, wide), value, 0.0)
                corr_ref[v : v + 1, c : c + wide] = jnp.sum(value, axis=0, keepdims=True)
        both.append(corr_ref[...])
    mine = jnp.where(row == 0, both[0], both[1])
    others = jnp.where(row == 0, both[1], both[0])
    correction = weight_ref[...] * (mine + pltpu.roll(others, shift, 1))
    corr_ref[...] = correction
    length = loop_out.shape[2]
    shown = pltpu.roll(correction, lax.rem(N - blk * length, N), 1)
    for v in range(count):
        loop_out[v] = shown[v : v + 1, :length]

    for v in range(count):
        for a in range(FOLD):
            for b in range(FOLD):
                after = src[v, a // 2, b // 2]
                x = u2s[v, a // 2, b // 2]
                gain = (after[:R] - x[:R], after[R:] - narrow(x)[1])
                edges = gain[1]
                for message, skip, half in (
                    (above, 0, sub < R // 2),
                    (below, FOLD - SECTIONS1, sub >= R // 2),
                ):
                    if skip <= a < skip + SECTIONS1:
                        at = (v * SECTIONS1 + a - skip) * FOLD + b
                        k = (2 * count + 1) * 4 + at // R
                        x = message[k, at % R : at % R + 1]
                        edges = edges + jnp.where(half, x, 0.0)
                start[v, a, b, :R] = u1[v, a, b] + gain[0]
                start[v, a, b, R:] = edges
    lane = lanes_of(2 * R, J)
    ring = lanes_of(2 * R, N)
    last = jnp.logical_and(lane == J - 1, row == 0)
    first = jnp.logical_and(lane == 0, row == 1)
    for a in range(FOLD):
        match = cells[a, :, :1] == ring
        for v in range(count):
            fix = jnp.where(match, corr_ref[v : v + 1], 0.0)
            fix = jnp.sum(fix, axis=1, keepdims=True)
            start[v, a, FOLD - 1] = start[v, a, FOLD - 1] + jnp.where(last, fix, 0.0)
            start[v, a, 0] = start[v, a, 0] + jnp.where(first, fix, 0.0)
    src = start
    for k in range(SECTIONS1):
        dst = (buf_a, buf_b)[k % 2]
        rows = R if k == SECTIONS1 - 1 else 2 * R
        section(dst, src, start, source, sigma, 1.0, 1.0 / (SECTIONS1 - k), FOLD, rows)
        src = dst
    for v in range(count):
        for a in range(FOLD):
            for b in range(FOLD):
                stage[v, b, pl.ds(a, R, stride=FOLD), :] = src[v, a, b, :R]
        for c, x in enumerate(join_lanes([stage[v, b] for b in range(FOLD)])):
            solution_ref[0, v, :, c * J : (c + 1) * J] = x


def body(state, forcing, sigma, partner, loop_weight, offset):
    _, count, rows, cols = state.shape
    R, J = rows // FOLD, cols // FOLD
    N = loop_weight.shape[1]
    blocks = lax.axis_size("blk")
    length = N // blocks
    real = functools.partial(jax.ShapeDtypeStruct, dtype=jnp.float32)
    near = lambda shape, dtype=jnp.float32: pltpu.VMEM(shape, dtype)
    away = lambda x: pltpu.with_memory_space_constraint(x, pltpu.HBM)
    held = lambda x: pltpu.with_memory_space_constraint(x, pltpu.VMEM)
    scratch = lambda *shape: pltpu.VMEM(shape, jnp.float32)
    far = pl.BlockSpec(memory_space=pltpu.HBM)
    slots = partner[:, :, 0]
    packed = near((-(-(edge_rows(count)[1] + 1) // 8) * 8, cols))
    limit = pltpu.CompilerParams(vmem_limit_bytes=LIMIT)
    head, tail, s_near, f_near, g_near, p_near = pl.pallas_call(
        pack_kernel,
        in_specs=[far] * 4,
        out_specs=[vmem()] * 6,
        out_shape=[
            packed,
            packed,
            near((count, rows, cols)),
            near((count, rows, cols)),
            near((rows, cols)),
            near((1, rows), jnp.int32),
        ],
        scratch_shapes=[pltpu.SemaphoreType.DMA((4,))],
        compiler_params=limit,
        name="pack",
    )(away(state), away(forcing), away(sigma), away(slots))
    up = [(i, (i + 1) % blocks) for i in range(blocks)]
    down = [((i + 1) % blocks, i) for i in range(blocks)]
    below = lax.ppermute(tail, "blk", up)
    above = lax.ppermute(head, "blk", down)

    st, fo, sg, own_slot = pl.pallas_call(
        fold_kernel,
        in_specs=[vmem()] * 4,
        out_specs=[vmem()] * 4,
        out_shape=[
            near((count, FOLD, FOLD, R, J)),
            near((count, FOLD, FOLD, R, J)),
            near((FOLD, FOLD, R, J)),
            near((FOLD, R, J), jnp.int32),
        ],
        scratch_shapes=[
            scratch(2 * count + 1, FOLD, rows, J),
            pltpu.VMEM((rows, J), jnp.int32),
        ],
        compiler_params=limit,
        name="fold",
    )(held(s_near), held(f_near), held(g_near), held(p_near))

    tiles = (2 * count + 1) * 4
    message = near((tiles - (-count * SECTIONS1 * FOLD // R), R, J))
    fine = (count, FOLD, FOLD, 2 * R, J)
    u1, source, sigma_w, cells, head, tail, loop = pl.pallas_call(
        down_kernel,
        in_specs=[vmem()] * 6,
        out_specs=[vmem()] * 7,
        out_shape=[
            near((count, FOLD, FOLD, R, J)),
            near(fine),
            near((FOLD, FOLD, 2 * R, J)),
            near((FOLD, 2 * R, J), jnp.int32),
            message,
            message,
            near((2 * blocks, J)),
        ],
        scratch_shapes=[
            scratch(*fine),
            scratch(*fine),
            scratch(*fine),
            scratch(2 * count + 1, FOLD, 2 * FOLD, J),
            scratch(2 * FOLD, cols),
            scratch(count, FOLD, FOLD, R, J),
            scratch(8, length),
        ],
        compiler_params=limit,
        name="down",
    )(held(st), held(fo), held(sg), held(own_slot), held(below), held(above))

    below = lax.ppermute(tail, "blk", up)
    above = lax.ppermute(head, "blk", down)
    loop = lax.all_to_all(loop, ("row", "blk"), 0, 0, tiled=True)

    mid = (count, 2, 2, 3 * R, J)
    low = (count, 1, 1, 3 * R, J)
    thin = (count, 2, 2, 2 * R, J)
    result, loop_out = pl.pallas_call(
        up_kernel,
        in_specs=[vmem()] * 8 + [far, pl.BlockSpec(memory_space=pltpu.SMEM)],
        out_specs=[vmem()] * 2,
        out_shape=[real(state.shape), real((count, 1, length))],
        scratch_shapes=[
            scratch(*mid), scratch(*mid), scratch(*mid[1:]), scratch(*mid),
            scratch(*low), scratch(*low), scratch(*low[1:]), scratch(*low),
            scratch(*mid), scratch(*mid), scratch(*low), scratch(*low),
            scratch(*thin), scratch(*thin), scratch(*thin[1:]), scratch(*thin), scratch(*thin),
            scratch(*fine), scratch(*fine), scratch(*fine),
            scratch(8, N),
            scratch(count, FOLD, rows, J),
            scratch(1, N),
            pltpu.SemaphoreType.DMA(()),
        ],
        compiler_params=limit,
        name="up",
    )(
        held(head), held(below), held(above), held(u1), held(source), held(sigma_w), held(cells),
        held(loop), away(loop_weight), offset,
    )
    return result, jnp.transpose(loop_out, (1, 0, 2))


def solution(mesh):
    placed = (
        P("row", None, "blk", None),
        P("row", None, "blk", None),
        P("row", "blk", None),
        P("row", "blk", None),
        P("row", None),
        P(),
    )

    return jax.shard_map(
        body,
        mesh=mesh,
        in_specs=placed,
        out_specs=(P("row", None, "blk", None), P("row", None, "blk")),
        check_vma=False,
    )
```

```python
import functools

import jax
import jax.numpy as jnp
from jax import lax
from jax.experimental import pallas as pl
from jax.experimental.pallas import tpu as pltpu
from jax.sharding import PartitionSpec as P


SECTIONS1 = 3
SECTIONS2 = 3
SECTIONS3 = 4
COEFF = 0.8

FOLD = 4
LIMIT = 24 * 1024 * 1024


def vmem():
    return pl.BlockSpec(memory_space=pltpu.VMEM)


def lanes_of(rows, cols):
    return lax.broadcasted_iota(jnp.int32, (rows, cols), 1)


def rows_of(rows, cols):
    return lax.broadcasted_iota(jnp.int32, (rows, cols), 0)


def pick(x, index):
    return jnp.take_along_axis(x, index, axis=1, mode="promise_in_bounds")


def split_lanes(x):
    rows, cols = x.shape
    wide = cols // FOLD
    run = wide // FOLD
    lane = lanes_of(rows, wide)
    parts = [x[:, c * wide : (c + 1) * wide] for c in range(FOLD)]
    group = lane // run
    out = []
    for b in range(FOLD):
        index = (lane % run) * FOLD + b
        taken = [pick(p, index) for p in parts]
        value = taken[-1]
        for c in range(FOLD - 1):
            value = jnp.where(group == c, taken[c], value)
        out.append(value)
    return out


def join_lanes(parts):
    rows, wide = parts[0].shape
    run = wide // FOLD
    lane = lanes_of(rows, wide)
    turn = lane % FOLD
    out = []
    for c in range(FOLD):
        index = lane // FOLD + c * run
        taken = [pick(p, index) for p in parts]
        value = taken[-1]
        for b in range(FOLD - 1):
            value = jnp.where(turn == b, taken[b], value)
        out.append(value)
    return out


def residual(src, source, diag, scale, a, b, fold, rows):
    count = src.shape[0]
    total, wide = src.shape[-2:]
    u = [src[v, a, b][:rows] for v in range(count)]
    q = u[0] * u[0]
    for v in range(1, count):
        q = q + u[v] * u[v]
    q = q * (1.0 / count)
    factor = diag + 0.5 * q / (1.0 + q)
    lane = lanes_of(rows, wide)
    out = []
    for v in range(count):
        up = src[v, a - 1, b] if a else pltpu.roll(src[v, fold - 1, b], 1, 0)
        down = src[v, a + 1, b] if a < fold - 1 else pltpu.roll(src[v, 0, b], total - 1, 0)
        if b:
            left = src[v, a, b - 1][:rows]
        else:
            left = jnp.where(lane == 0, 0.0, pltpu.roll(src[v, a, fold - 1][:rows], 1, 1))
        if b < fold - 1:
            right = src[v, a, b + 1][:rows]
        else:
            right = jnp.where(lane == wide - 1, 0.0, pltpu.roll(src[v, a, 0][:rows], wide - 1, 1))
        near = (up[:rows] + down[:rows]) + (left + right)
        out.append(source[v, a, b][:rows] + scale * near - factor * u[v])
    return out


def section(dst, src, start, source, sigma, tau, scale, weight, fold, rows):
    for a in range(fold):
        for b in range(fold):
            diag = 4.0 * scale + sigma[a, b][:rows]
            step = weight * tau[a, b][:rows]
            res = residual(src, source, diag, scale, a, b, fold, rows)
            for v, r in enumerate(res):
                dst[v, a, b, :rows] = start[v, a, b][:rows] + step * r


def first_section(dst, start, coarse, tau, weight, fold):
    for a in range(fold):
        for b in range(fold):
            step = weight * tau[a, b]
            for v in range(dst.shape[0]):
                dst[v, a, b] = start[v, a, b] + step * coarse[v, a, b]


def step_size(sigma, scale):
    return COEFF / (4.0 * scale + sigma + 1.5)


def fine_residual(src, edge, source, diag, b, a=None):
    count = src.shape[0]
    R, J = src.shape[-2:]
    sub, lane = rows_of(R, J), lanes_of(R, J)
    top = FOLD - 1
    at = (lambda v, i: edge[v, i]) if a is None else (lambda v, i: src[v, a, i])
    u = [at(v, b) for v in range(count)]
    q = u[0] * u[0]
    for v in range(1, count):
        q = q + u[v] * u[v]
    q = q * (1.0 / count)
    factor = diag + 0.5 * q / (1.0 + q)
    out = []
    for v in range(count):
        if a is None:
            up = jnp.where(sub == FOLD, src[v, top, b, R - 1 :], pltpu.roll(u[v], 1, 0))
            down = jnp.where(sub == top, src[v, 0, b, :1], pltpu.roll(u[v], R - 1, 0))
        else:
            if a:
                up = src[v, a - 1, b]
            else:
                up = jnp.where(sub == 0, edge[v, b, top : top + 1], pltpu.roll(src[v, top, b], 1, 0))
            if a < top:
                down = src[v, a + 1, b]
            else:
                below = edge[v, b, FOLD : FOLD + 1]
                down = jnp.where(sub == R - 1, below, pltpu.roll(src[v, 0, b], R - 1, 0))
        left = at(v, b - 1) if b else jnp.where(lane == 0, 0.0, pltpu.roll(at(v, top), 1, 1))
        right = at(v, b + 1) if b < top else jnp.where(lane == J - 1, 0.0, pltpu.roll(at(v, 0), J - 1, 1))
        near = (up + down) + (left + right)
        out.append((source[v, b] if a is None else source[v, a, b]) + near - factor * u[v])
    return out


def fine_section(dst, dst_edge, src, edge, start, start_edge, source, source_edge, sigma, tau, weight):
    for a in range(FOLD + 1):
        if a == FOLD and dst_edge is None:
            continue
        for b in range(FOLD):
            diag = 4.0 + sigma[a, b]
            step = weight * tau[a, b]
            if a == FOLD:
                res = fine_residual(src, edge, source_edge, diag, b)
            else:
                res = fine_residual(src, edge, source, diag, b, a)
            for v, r in enumerate(res):
                if a == FOLD:
                    dst_edge[v, b] = start_edge[v, b] + step * r
                else:
                    dst[v, a, b] = start[v, a, b] + step * r


def quarter(x):
    return 0.25 * ((x(0, 0) + x(0, 1)) + (x(1, 0) + x(1, 1)))


def wrap(x, size):
    return x & (size - 1) if size & (size - 1) == 0 else lax.rem(x, size)


def fetch(pairs, sems):
    copies = [pltpu.make_async_copy(x, y, sems.at[k]) for k, (x, y) in enumerate(pairs)]
    for copy in copies:
        copy.start()
    for copy in copies:
        copy.wait()


def edge_rows(count):
    out = []
    at = 0
    for kind, width in ((0, SECTIONS1 + 1), (1, SECTIONS1), (2, SECTIONS1)):
        for v in range(1 if kind == 2 else count):
            out.append((kind, v, at, width))
            at += width
    return out, at


def pack_kernel(s_hbm, f_hbm, g_hbm, p_hbm, head, tail, s_ref, f_ref, g_ref, p_ref, sems):
    count, rows = s_ref.shape[:2]
    fetch(((p_hbm, p_ref), (s_hbm.at[0], s_ref), (f_hbm.at[0], f_ref), (g_hbm.at[0], g_ref)), sems)
    places, end = edge_rows(count)
    for kind, v, at, width in places:
        x = g_ref if kind == 2 else (s_ref, f_ref)[kind].at[v]
        head[at : at + width] = x[:width]
        tail[at : at + width] = x[rows - width :]
    for message in (head, tail):
        message[end:] = jnp.zeros((message.shape[0] - end, message.shape[1]), jnp.float32)
        message[end : end + 1, :rows] = p_ref[...].astype(jnp.float32)


def fold_kernel(s_ref, f_ref, g_ref, p_ref, st, fo, sg, own_slot, stage, slots):
    count = st.shape[0]
    R, _ = st.shape[-2:]
    rows = s_ref.shape[1]
    for ch in range(2 * count + 1):
        kind, v = divmod(ch, count)
        x = g_ref[...] if kind == 2 else (s_ref, f_ref)[kind][v]
        for b, part in enumerate(split_lanes(x)):
            stage[ch, b] = part
        for a in range(FOLD):
            for b in range(FOLD):
                part = stage[ch, b, pl.ds(a, R, stride=FOLD), :]
                if kind == 2:
                    sg[a, b] = part
                else:
                    (st, fo)[kind][v, a, b] = part
    diagonal = lanes_of(rows, rows) == rows_of(rows, rows)
    column = jnp.where(diagonal, p_ref[...].astype(jnp.float32), 0.0)
    column = jnp.sum(column, axis=1, keepdims=True).astype(jnp.int32)
    slots[...] = jnp.broadcast_to(column, slots.shape)
    for a in range(FOLD):
        own_slot[a] = slots[pl.ds(a, R, stride=FOLD), :]


def down_kernel(
    st, fo, sg, own_slot, below, above,
    u1, edges, sigma, tau, cells, head, tail, loop,
    buf_a, buf_b, edge_a, edge_b, box, resid, own_loop,
):
    count = st.shape[0]
    R, J = st.shape[-2:]
    row = lax.axis_index("row")
    blk = lax.axis_index("blk")
    blocks = lax.axis_size("blk")
    slots = own_loop.shape[1]
    N = blocks * slots
    rows = R * FOLD
    sub = rows_of(R, J)
    places, end = edge_rows(count)
    for ch, (kind, v, at, width) in enumerate(places):
        if width < FOLD:
            box[...] = jnp.zeros_like(box)
        box[FOLD - width : FOLD] = below[at : at + width]
        box[FOLD : FOLD + width] = above[at : at + width]
        for b, part in enumerate(split_lanes(box[...])):
            edges[ch, b] = part
    for b in range(FOLD):
        for a in range(FOLD):
            sigma[a, b] = sg[a, b]
            tau[a, b] = step_size(sg[a, b], 1.0)
        sigma[FOLD, b] = edges[2 * count, b]
        tau[FOLD, b] = step_size(edges[2 * count, b], 1.0)

    place = lanes_of(1, rows)
    high = lax.rem(blk + 1, blocks)
    low = lax.rem(blk + blocks - 1, blocks)
    column = jnp.zeros((R, J), jnp.int32)
    for k in range(2 * FOLD):
        message, i = (below, rows - FOLD + k) if k < FOLD else (above, k - FOLD)
        x = jnp.where(place == i, message[end : end + 1, :rows], 0.0)
        x = jnp.sum(x, axis=1, keepdims=True).astype(jnp.int32)
        column = jnp.where(sub == k, jnp.broadcast_to(x, (R, J)), column)
    cells[FOLD] = wrap(column * blocks + jnp.where(sub < FOLD, low, high), N)
    for a in range(FOLD):
        cells[a] = wrap(own_slot[a] * blocks + blk, N)

    start_edge = edges.at[:count]
    source_edge = edges.at[count : 2 * count]
    src, edge = st, start_edge
    for k in range(SECTIONS1):
        dst = u1 if k == SECTIONS1 - 1 else (buf_a, buf_b)[k % 2]
        dst_edge = (edge_a, edge_b)[k % 2]
        fine_section(
            dst, dst_edge, src, edge, st, start_edge, fo, source_edge, sigma, tau, 1.0 / (SECTIONS1 - k)
        )
        src, edge = dst, dst_edge

    first = (2 * count + 1) * 4 * R
    for a in range(FOLD):
        for b in range(FOLD):
            res = fine_residual(u1, edge, fo, 4.0 + sigma[a, b], b, a)
            for v in range(count):
                resid[v, a, b] = res[v]
                at = first + (v * FOLD + b) * SECTIONS1 + a
                if a < SECTIONS1:
                    head[at : at + 1] = u1[v, a, b, :1]
                at -= FOLD - SECTIONS1
                if a >= FOLD - SECTIONS1:
                    tail[at : at + 1] = u1[v, a, b, R - 1 :]
    for a in range(2):
        for b in range(2):
            for v in range(count):
                at = ((v * 2 + a) * 2 + b) * R
                x = quarter(lambda i, j: u1[v, 2 * a + i, 2 * b + j])
                head[at : at + R] = x
                tail[at : at + R] = x
                at += 4 * count * R
                x = quarter(lambda i, j: resid[v, 2 * a + i, 2 * b + j])
                head[at : at + R] = x
                tail[at : at + R] = x
            at = (8 * count + a * 2 + b) * R
            x = quarter(lambda i, j: sg[2 * a + i, 2 * b + j])
            head[at : at + R] = x
            tail[at : at + R] = x

    lane = lanes_of(R, J)
    column = jnp.where(row == 0, J - 1, 0)
    sums = jnp.zeros((R, J), jnp.float32)
    for a in range(FOLD):
        slot = wrap(own_slot[a], slots)
        for v in range(count):
            face = jnp.where(row == 0, resid[v, a, FOLD - 1], resid[v, a, 0])
            face = jnp.sum(jnp.where(lane == column, face, 0.0), axis=1, keepdims=True)
            sums = sums + jnp.where(lane == slot + v * slots, face, 0.0)
    loop[...] = jnp.broadcast_to(jnp.sum(sums, axis=0, keepdims=True), loop.shape)


def up_kernel(
    own, below, above, u1, source, edges, sigma, tau, cells, loop, weight_hbm, offset_ref,
    solution_ref, loop_out,
    u2s, r2s, s2, t2, f2, u3s, r3s, s3, t3, f3, buf2a, buf2b, buf3a, buf3b,
    n2, nf2, ns2, nt2, mid_a, mid_b, start, buf_a, buf_b, edge, edge_a, edge_b,
    corr_ref, stage, weight_ref, sem,
):
    count = u1.shape[0]
    R, J = u1.shape[-2:]
    N = corr_ref.shape[1]
    row = lax.axis_index("row")
    blk = lax.axis_index("blk")
    blocks = lax.axis_size("blk")
    sub = rows_of(R, J)
    weights = pltpu.make_async_copy(weight_hbm, weight_ref, sem)
    weights.start()

    for at in range(8 * count + 4):
        if at < 8 * count:
            kind, rest = divmod(at, 4 * count)
            v, ab = divmod(rest, 4)
            a, b = divmod(ab, 2)
            dst = (u2s, r2s)[kind].at[v, a, b]
        else:
            a, b = divmod(at - 8 * count, 2)
            dst = s2.at[a, b]
        for part, message in enumerate((own, above, below)):
            dst[part * R : (part + 1) * R] = message[at * R : (at + 1) * R]

    for a in range(2):
        for b in range(2):
            t2[a, b] = step_size(s2[a, b], 0.25)
            res = residual(u2s, r2s, 1.0 + s2[a, b], 0.25, a, b, 2, 3 * R)
            for v in range(count):
                f2[v, a, b] = 2.0 * r2s[v, a, b] - res[v]
    first_section(buf2a, u2s, r2s, t2, 1.0 / SECTIONS2, 2)
    src, dst = buf2a, buf2b
    for k in range(1, SECTIONS2):
        section(dst, src, u2s, f2, s2, t2, 0.25, 1.0 / (SECTIONS2 - k), 2, 3 * R)
        src, dst = dst, src
    u2, r2 = src, dst
    for a in range(2):
        for b in range(2):
            res = residual(u2, f2, 1.0 + s2[a, b], 0.25, a, b, 2, 3 * R)
            for v in range(count):
                r2[v, a, b] = res[v]
    for v in range(count):
        u3s[v, 0, 0] = quarter(lambda i, j: u2[v, i, j])
        r3s[v, 0, 0] = quarter(lambda i, j: r2[v, i, j])
    s3[0, 0] = quarter(lambda i, j: s2[i, j])
    t3[0, 0] = step_size(s3[0, 0], 0.0625)

    res = residual(u3s, r3s, 0.25 + s3[0, 0], 0.0625, 0, 0, 1, 3 * R)
    for v in range(count):
        f3[v, 0, 0] = 2.0 * r3s[v, 0, 0] - res[v]
    first_section(buf3a, u3s, r3s, t3, 1.0 / SECTIONS3, 1)
    src3, dst3 = buf3a, buf3b
    for k in range(1, SECTIONS3):
        section(dst3, src3, u3s, f3, s3, t3, 0.0625, 1.0 / (SECTIONS3 - k), 1, 3 * R)
        src3, dst3 = dst3, src3

    def narrow(x):
        return x[:R], jnp.where(sub < R // 2, x[R : 2 * R], x[2 * R :])

    for v in range(count):
        gain = narrow(src3[v, 0, 0] - u3s[v, 0, 0])
        for a in range(2):
            for b in range(2):
                for part in range(2):
                    at = slice(part * R, (part + 1) * R)
                    n2[v, a, b, at] = narrow(u2[v, a, b])[part] + gain[part]
                    nf2[v, a, b, at] = narrow(f2[v, a, b])[part]
                    if v == 0:
                        ns2[a, b, at] = narrow(s2[a, b])[part]
                        nt2[a, b, at] = narrow(t2[a, b])[part]
    src = n2
    for k in range(SECTIONS2):
        dst = (mid_a, mid_b)[k % 2]
        section(dst, src, n2, nf2, ns2, nt2, 0.25, 1.0 / (SECTIONS2 - k), 2, 2 * R)
        src = dst

    slots = N // blocks
    wide = loop.shape[1]
    offset = offset_ref[0]
    shift = lax.rem(jnp.where(row == 0, N - offset, offset), N)
    weights.wait()
    both = []
    for r in range(2):
        held = loop[r * blocks : (r + 1) * blocks]
        for v in range(count):
            for c in range(0, N, wide):
                cell = lanes_of(blocks, wide) + c
                value = pick(held, cell // blocks + v * slots)
                value = jnp.where(wrap(cell, blocks) == rows_of(blocks, wide), value, 0.0)
                corr_ref[v : v + 1, c : c + wide] = jnp.sum(value, axis=0, keepdims=True)
        both.append(corr_ref[...])
    mine = jnp.where(row == 0, both[0], both[1])
    others = jnp.where(row == 0, both[1], both[0])
    correction = weight_ref[...] * (mine + pltpu.roll(others, shift, 1))
    corr_ref[...] = correction
    length = loop_out.shape[2]
    shown = pltpu.roll(correction, lax.rem(N - blk * length, N), 1)
    for v in range(count):
        loop_out[v] = shown[v : v + 1, :length]

    first = (2 * count + 1) * 4 * R
    for v in range(count):
        for b in range(2):
            rim = {}
            for a in range(2):
                x, after = u2s[v, a, b], src[v, a, b]
                gain = after[:R] - x[:R]
                rim[0, a] = src[v, a, b, 2 * R - 1 :] - u2s[v, a, b, 3 * R - 1 :]
                rim[1, a] = src[v, a, b, R : R + 1] - u2s[v, a, b, R : R + 1]
                for i in range(2):
                    for j in range(2):
                        at = (v, 2 * a + i, 2 * b + j)
                        start[at] = u1[at] + gain
            lower = jnp.where(sub < FOLD // 2, rim[0, 0], rim[0, 1])
            upper = jnp.where(sub < FOLD + FOLD // 2, rim[1, 0], rim[1, 1])
            gain = jnp.where(sub < FOLD, lower, upper)
            for j in range(2):
                tile = edge.at[v, 2 * b + j]
                tile[...] = jnp.zeros((R, J), jnp.float32)
                at = first + (v * FOLD + 2 * b + j) * SECTIONS1
                tile[FOLD - SECTIONS1 : FOLD] = below[at : at + SECTIONS1]
                tile[FOLD : FOLD + SECTIONS1] = above[at : at + SECTIONS1]
                tile[...] = tile[...] + gain
    lane = lanes_of(R, J)
    ring = lanes_of(R, N)
    last = jnp.logical_and(lane == J - 1, row == 0)
    nearest = jnp.logical_and(lane == 0, row == 1)
    for a in range(FOLD + 1):
        match = cells[a, :, :1] == ring
        for v in range(count):
            fix = jnp.where(match, corr_ref[v : v + 1], 0.0)
            fix = jnp.sum(fix, axis=1, keepdims=True)
            tiles = edge.at[v] if a == FOLD else start.at[v, a]
            tiles[FOLD - 1] = tiles[FOLD - 1] + jnp.where(last, fix, 0.0)
            tiles[0] = tiles[0] + jnp.where(nearest, fix, 0.0)
    source_edge = edges.at[count : 2 * count]
    src, src_edge = start, edge
    for k in range(SECTIONS1):
        dst = (buf_a, buf_b)[k % 2]
        dst_edge = None if k == SECTIONS1 - 1 else (edge_a, edge_b)[k % 2]
        fine_section(
            dst, dst_edge, src, src_edge, start, edge, source, source_edge, sigma, tau,
            1.0 / (SECTIONS1 - k),
        )
        src, src_edge = dst, dst_edge
    for v in range(count):
        for a in range(FOLD):
            for b in range(FOLD):
                stage[v, b, pl.ds(a, R, stride=FOLD), :] = src[v, a, b]
        for c, x in enumerate(join_lanes([stage[v, b] for b in range(FOLD)])):
            solution_ref[0, v, :, c * J : (c + 1) * J] = x


def body(state, forcing, sigma, partner, loop_weight, offset):
    _, count, rows, cols = state.shape
    R, J = rows // FOLD, cols // FOLD
    N = loop_weight.shape[1]
    blocks = lax.axis_size("blk")
    length = N // blocks
    real = functools.partial(jax.ShapeDtypeStruct, dtype=jnp.float32)
    near = lambda shape, dtype=jnp.float32: pltpu.VMEM(shape, dtype)
    away = lambda x: pltpu.with_memory_space_constraint(x, pltpu.HBM)
    held = lambda x: pltpu.with_memory_space_constraint(x, pltpu.VMEM)
    scratch = lambda *shape: pltpu.VMEM(shape, jnp.float32)
    far = pl.BlockSpec(memory_space=pltpu.HBM)
    slots = partner[:, :, 0]
    packed = near((-(-(edge_rows(count)[1] + 1) // 8) * 8, cols))
    limit = pltpu.CompilerParams(vmem_limit_bytes=LIMIT)
    head, tail, s_near, f_near, g_near, p_near = pl.pallas_call(
        pack_kernel,
        in_specs=[far] * 4,
        out_specs=[vmem()] * 6,
        out_shape=[
            packed,
            packed,
            near((count, rows, cols)),
            near((count, rows, cols)),
            near((rows, cols)),
            near((1, rows), jnp.int32),
        ],
        scratch_shapes=[pltpu.SemaphoreType.DMA((4,))],
        compiler_params=limit,
        name="pack",
    )(away(state), away(forcing), away(sigma), away(slots))
    up = [(i, (i + 1) % blocks) for i in range(blocks)]
    down = [((i + 1) % blocks, i) for i in range(blocks)]
    below = lax.ppermute(tail, "blk", up)
    above = lax.ppermute(head, "blk", down)

    st, fo, sg, own_slot = pl.pallas_call(
        fold_kernel,
        in_specs=[vmem()] * 4,
        out_specs=[vmem()] * 4,
        out_shape=[
            near((count, FOLD, FOLD, R, J)),
            near((count, FOLD, FOLD, R, J)),
            near((FOLD, FOLD, R, J)),
            near((FOLD, R, J), jnp.int32),
        ],
        scratch_shapes=[
            scratch(2 * count + 1, FOLD, rows, J),
            pltpu.VMEM((rows, J), jnp.int32),
        ],
        compiler_params=limit,
        name="fold",
    )(held(s_near), held(f_near), held(g_near), held(p_near))

    far_rows = (2 * count + 1) * 4 * R + count * SECTIONS1 * FOLD
    message = near((-(-far_rows // 8) * 8, J))
    fine = (count, FOLD, FOLD, R, J)
    rim = (count, FOLD, R, J)
    u1, edges, sigma_w, tau, cells, head, tail, loop = pl.pallas_call(
        down_kernel,
        in_specs=[vmem()] * 6,
        out_specs=[vmem()] * 8,
        out_shape=[
            near(fine),
            near((2 * count + 1, FOLD, R, J)),
            near((FOLD + 1, FOLD, R, J)),
            near((FOLD + 1, FOLD, R, J)),
            near((FOLD + 1, R, J), jnp.int32),
            message,
            message,
            near((2 * blocks, J)),
        ],
        scratch_shapes=[
            scratch(*fine),
            scratch(*fine),
            scratch(*rim),
            scratch(*rim),
            scratch(2 * FOLD, cols),
            scratch(*fine),
            scratch(8, length),
        ],
        compiler_params=limit,
        name="down",
    )(held(st), held(fo), held(sg), held(own_slot), held(below), held(above))

    below = lax.ppermute(tail, "blk", up)
    above = lax.ppermute(head, "blk", down)
    loop = lax.all_to_all(loop, ("row", "blk"), 0, 0, tiled=True)

    mid = (count, 2, 2, 3 * R, J)
    low = (count, 1, 1, 3 * R, J)
    thin = (count, 2, 2, 2 * R, J)
    result, loop_out = pl.pallas_call(
        up_kernel,
        in_specs=[vmem()] * 10 + [far, pl.BlockSpec(memory_space=pltpu.SMEM)],
        out_specs=[vmem()] * 2,
        out_shape=[real(state.shape), real((count, 1, length))],
        scratch_shapes=[
            scratch(*mid), scratch(*mid), scratch(*mid[1:]), scratch(*mid[1:]), scratch(*mid),
            scratch(*low), scratch(*low), scratch(*low[1:]), scratch(*low[1:]), scratch(*low),
            scratch(*mid), scratch(*mid), scratch(*low), scratch(*low),
            scratch(*thin), scratch(*thin), scratch(*thin[1:]), scratch(*thin[1:]),
            scratch(*thin), scratch(*thin),
            scratch(*fine), scratch(*fine), scratch(*fine),
            scratch(*rim), scratch(*rim), scratch(*rim),
            scratch(8, N),
            scratch(count, FOLD, rows, J),
            scratch(1, N),
            pltpu.SemaphoreType.DMA(()),
        ],
        compiler_params=limit,
        name="up",
    )(
        held(head), held(below), held(above), held(u1), held(fo), held(edges), held(sigma_w),
        held(tau), held(cells), held(loop), away(loop_weight), offset,
    )
    return result, jnp.transpose(loop_out, (1, 0, 2))


def solution(mesh):
    placed = (
        P("row", None, "blk", None),
        P("row", None, "blk", None),
        P("row", "blk", None),
        P("row", "blk", None),
        P("row", None),
        P(),
    )

    return jax.shard_map(
        body,
        mesh=mesh,
        in_specs=placed,
        out_specs=(P("row", None, "blk", None), P("row", None, "blk")),
        check_vma=False,
    )
```

```python
import functools

import jax
import jax.numpy as jnp
from jax import lax
from jax.experimental import pallas as pl
from jax.experimental.pallas import tpu as pltpu
from jax.sharding import PartitionSpec as P


SECTIONS1 = 3
SECTIONS2 = 3
SECTIONS3 = 4
COEFF = 0.8

FOLD = 4
LIMIT = 24 * 1024 * 1024


def vmem():
    return pl.BlockSpec(memory_space=pltpu.VMEM)


def lanes_of(rows, cols):
    return lax.broadcasted_iota(jnp.int32, (rows, cols), 1)


def rows_of(rows, cols):
    return lax.broadcasted_iota(jnp.int32, (rows, cols), 0)


def pick(x, index):
    return jnp.take_along_axis(x, index, axis=1, mode="promise_in_bounds")


def split_lanes(x):
    rows, cols = x.shape
    wide = cols // FOLD
    run = wide // FOLD
    lane = lanes_of(rows, wide)
    parts = [x[:, c * wide : (c + 1) * wide] for c in range(FOLD)]
    group = lane // run
    out = []
    for b in range(FOLD):
        index = (lane % run) * FOLD + b
        taken = [pick(p, index) for p in parts]
        value = taken[-1]
        for c in range(FOLD - 1):
            value = jnp.where(group == c, taken[c], value)
        out.append(value)
    return out


def join_lanes(parts):
    rows, wide = parts[0].shape
    run = wide // FOLD
    lane = lanes_of(rows, wide)
    turn = lane % FOLD
    out = []
    for c in range(FOLD):
        index = lane // FOLD + c * run
        taken = [pick(p, index) for p in parts]
        value = taken[-1]
        for b in range(FOLD - 1):
            value = jnp.where(turn == b, taken[b], value)
        out.append(value)
    return out


def residual(src, source, diag, scale, a, b, fold, rows):
    count = src.shape[0]
    total, wide = src.shape[-2:]
    u = [src[v, a, b][:rows] for v in range(count)]
    q = u[0] * u[0]
    for v in range(1, count):
        q = q + u[v] * u[v]
    q = q * (1.0 / count)
    factor = diag + 0.5 * q / (1.0 + q)
    lane = lanes_of(rows, wide)
    out = []
    for v in range(count):
        up = src[v, a - 1, b] if a else pltpu.roll(src[v, fold - 1, b], 1, 0)
        down = src[v, a + 1, b] if a < fold - 1 else pltpu.roll(src[v, 0, b], total - 1, 0)
        if b:
            left = src[v, a, b - 1][:rows]
        else:
            left = jnp.where(lane == 0, 0.0, pltpu.roll(src[v, a, fold - 1][:rows], 1, 1))
        if b < fold - 1:
            right = src[v, a, b + 1][:rows]
        else:
            right = jnp.where(lane == wide - 1, 0.0, pltpu.roll(src[v, a, 0][:rows], wide - 1, 1))
        near = (up[:rows] + down[:rows]) + (left + right)
        out.append(source[v, a, b][:rows] + scale * near - factor * u[v])
    return out


def section(dst, src, start, source, sigma, tau, scale, weight, fold, rows):
    for a in range(fold):
        for b in range(fold):
            diag = 4.0 * scale + sigma[a, b][:rows]
            step = weight * tau[a, b][:rows]
            res = residual(src, source, diag, scale, a, b, fold, rows)
            for v, r in enumerate(res):
                dst[v, a, b, :rows] = start[v, a, b][:rows] + step * r


def first_section(dst, start, coarse, tau, weight, fold):
    for a in range(fold):
        for b in range(fold):
            step = weight * tau[a, b]
            for v in range(dst.shape[0]):
                dst[v, a, b] = start[v, a, b] + step * coarse[v, a, b]


def step_size(sigma, scale):
    return COEFF / (4.0 * scale + sigma + 1.5)


def fine_residual(src, edge, source, diag, b, a=None):
    count = src.shape[0]
    R, J = src.shape[-2:]
    sub, lane = rows_of(R, J), lanes_of(R, J)
    top = FOLD - 1
    at = (lambda v, i: edge[v, i]) if a is None else (lambda v, i: src[v, a, i])
    u = [at(v, b) for v in range(count)]
    q = u[0] * u[0]
    for v in range(1, count):
        q = q + u[v] * u[v]
    q = q * (1.0 / count)
    factor = diag + 0.5 * q / (1.0 + q)
    out = []
    for v in range(count):
        if a is None:
            up = jnp.where(sub == FOLD, src[v, top, b, R - 1 :], pltpu.roll(u[v], 1, 0))
            down = jnp.where(sub == top, src[v, 0, b, :1], pltpu.roll(u[v], R - 1, 0))
        else:
            if a:
                up = src[v, a - 1, b]
            else:
                up = jnp.where(sub == 0, edge[v, b, top : top + 1], pltpu.roll(src[v, top, b], 1, 0))
            if a < top:
                down = src[v, a + 1, b]
            else:
                below = edge[v, b, FOLD : FOLD + 1]
                down = jnp.where(sub == R - 1, below, pltpu.roll(src[v, 0, b], R - 1, 0))
        left = at(v, b - 1) if b else jnp.where(lane == 0, 0.0, pltpu.roll(at(v, top), 1, 1))
        right = at(v, b + 1) if b < top else jnp.where(lane == J - 1, 0.0, pltpu.roll(at(v, 0), J - 1, 1))
        near = (up + down) + (left + right)
        out.append((source[v, b] if a is None else source[v, a, b]) + near - factor * u[v])
    return out


def fine_section(dst, dst_edge, src, edge, start, start_edge, source, source_edge, sigma, tau, weight,
                 groups=range(FOLD)):
    for a in range(FOLD + 1):
        if a == FOLD and dst_edge is None:
            continue
        for b in groups:
            diag = 4.0 + sigma[a, b]
            step = weight * tau[a, b]
            if a == FOLD:
                res = fine_residual(src, edge, source_edge, diag, b)
            else:
                res = fine_residual(src, edge, source, diag, b, a)
            for v, r in enumerate(res):
                if a == FOLD:
                    dst_edge[v, b] = start_edge[v, b] + step * r
                else:
                    dst[v, a, b] = start[v, a, b] + step * r


class Mixed:
    def __init__(self, base, fresh, groups, axis):
        self.base, self.fresh, self.groups, self.axis = base, fresh, groups, axis
        self.shape = base.shape

    def __getitem__(self, at):
        return (self.fresh if at[self.axis] in self.groups else self.base)[at]


def quarter(x):
    return 0.25 * ((x(0, 0) + x(0, 1)) + (x(1, 0) + x(1, 1)))


def wrap(x, size):
    return x & (size - 1) if size & (size - 1) == 0 else lax.rem(x, size)


def fetch(pairs, sems):
    copies = [pltpu.make_async_copy(x, y, sems.at[k]) for k, (x, y) in enumerate(pairs)]
    for copy in copies:
        copy.start()
    for copy in copies:
        copy.wait()


def edge_rows(count):
    out = []
    at = 0
    for kind, width in ((0, SECTIONS1 + 1), (1, SECTIONS1), (2, SECTIONS1)):
        for v in range(1 if kind == 2 else count):
            out.append((kind, v, at, width))
            at += width
    return out, at


def pack_kernel(
    s_hbm, f_hbm, g_hbm, p_hbm, w_hbm, head, tail, s_ref, f_ref, g_ref, p_ref, w_ref, sems
):
    count, rows = s_ref.shape[:2]
    fetch(
        (
            (p_hbm, p_ref), (w_hbm, w_ref), (s_hbm.at[0], s_ref), (f_hbm.at[0], f_ref),
            (g_hbm.at[0], g_ref),
        ),
        sems,
    )
    places, end = edge_rows(count)
    for kind, v, at, width in places:
        x = g_ref if kind == 2 else (s_ref, f_ref)[kind].at[v]
        head[at : at + width] = x[:width]
        tail[at : at + width] = x[rows - width :]
    for message in (head, tail):
        message[end:] = jnp.zeros((message.shape[0] - end, message.shape[1]), jnp.float32)
        message[end : end + 1, :rows] = p_ref[...].astype(jnp.float32)


def fold_kernel(s_ref, f_ref, g_ref, p_ref, st, fo, sg, own_slot, stage, slots):
    count = st.shape[0]
    R, _ = st.shape[-2:]
    rows = s_ref.shape[1]
    for ch in range(2 * count + 1):
        kind, v = divmod(ch, count)
        x = g_ref[...] if kind == 2 else (s_ref, f_ref)[kind][v]
        for b, part in enumerate(split_lanes(x)):
            stage[ch, b] = part
        for a in range(FOLD):
            for b in range(FOLD):
                part = stage[ch, b, pl.ds(a, R, stride=FOLD), :]
                if kind == 2:
                    sg[a, b] = part
                else:
                    (st, fo)[kind][v, a, b] = part
    diagonal = lanes_of(rows, rows) == rows_of(rows, rows)
    column = jnp.where(diagonal, p_ref[...].astype(jnp.float32), 0.0)
    column = jnp.sum(column, axis=1, keepdims=True).astype(jnp.int32)
    slots[...] = jnp.broadcast_to(column, slots.shape)
    for a in range(FOLD):
        own_slot[a] = slots[pl.ds(a, R, stride=FOLD), :]


def down_kernel(
    st, fo, sg, own_slot, below, above,
    u1, edges, sigma, tau, cells, head, tail, loop,
    buf_a, buf_b, edge_a, edge_b, box, resid, own_loop,
):
    count = st.shape[0]
    R, J = st.shape[-2:]
    row = lax.axis_index("row")
    blk = lax.axis_index("blk")
    blocks = lax.axis_size("blk")
    slots = own_loop.shape[1]
    N = blocks * slots
    rows = R * FOLD
    sub = rows_of(R, J)
    places, end = edge_rows(count)
    for ch, (kind, v, at, width) in enumerate(places):
        if width < FOLD:
            box[...] = jnp.zeros_like(box)
        box[FOLD - width : FOLD] = below[at : at + width]
        box[FOLD : FOLD + width] = above[at : at + width]
        for b, part in enumerate(split_lanes(box[...])):
            edges[ch, b] = part
    for b in range(FOLD):
        for a in range(FOLD):
            sigma[a, b] = sg[a, b]
            tau[a, b] = step_size(sg[a, b], 1.0)
        sigma[FOLD, b] = edges[2 * count, b]
        tau[FOLD, b] = step_size(edges[2 * count, b], 1.0)

    place = lanes_of(1, rows)
    high = lax.rem(blk + 1, blocks)
    low = lax.rem(blk + blocks - 1, blocks)
    column = jnp.zeros((R, J), jnp.int32)
    for k in range(2 * FOLD):
        message, i = (below, rows - FOLD + k) if k < FOLD else (above, k - FOLD)
        x = jnp.where(place == i, message[end : end + 1, :rows], 0.0)
        x = jnp.sum(x, axis=1, keepdims=True).astype(jnp.int32)
        column = jnp.where(sub == k, jnp.broadcast_to(x, (R, J)), column)
    cells[FOLD] = wrap(column * blocks + jnp.where(sub < FOLD, low, high), N)
    for a in range(FOLD):
        cells[a] = wrap(own_slot[a] * blocks + blk, N)

    start_edge = edges.at[:count]
    source_edge = edges.at[count : 2 * count]
    src, edge = st, start_edge
    for k in range(SECTIONS1):
        dst = u1 if k == SECTIONS1 - 1 else (buf_a, buf_b)[k % 2]
        dst_edge = (edge_a, edge_b)[k % 2]
        fine_section(
            dst, dst_edge, src, edge, st, start_edge, fo, source_edge, sigma, tau, 1.0 / (SECTIONS1 - k)
        )
        src, edge = dst, dst_edge

    first = (2 * count + 1) * 4 * R
    for a in range(FOLD):
        for b in range(FOLD):
            res = fine_residual(u1, edge, fo, 4.0 + sigma[a, b], b, a)
            for v in range(count):
                resid[v, a, b] = res[v]
                at = first + (v * FOLD + b) * SECTIONS1 + a
                if a < SECTIONS1:
                    head[at : at + 1] = u1[v, a, b, :1]
                at -= FOLD - SECTIONS1
                if a >= FOLD - SECTIONS1:
                    tail[at : at + 1] = u1[v, a, b, R - 1 :]
    for a in range(2):
        for b in range(2):
            for v in range(count):
                at = ((v * 2 + a) * 2 + b) * R
                x = quarter(lambda i, j: u1[v, 2 * a + i, 2 * b + j])
                head[at : at + R] = x
                tail[at : at + R] = x
                at += 4 * count * R
                x = quarter(lambda i, j: resid[v, 2 * a + i, 2 * b + j])
                head[at : at + R] = x
                tail[at : at + R] = x
            at = (8 * count + a * 2 + b) * R
            x = quarter(lambda i, j: sg[2 * a + i, 2 * b + j])
            head[at : at + R] = x
            tail[at : at + R] = x

    lane = lanes_of(R, J)
    column = jnp.where(row == 0, J - 1, 0)
    sums = jnp.zeros((R, J), jnp.float32)
    for a in range(FOLD):
        slot = wrap(own_slot[a], slots)
        for v in range(count):
            face = jnp.where(row == 0, resid[v, a, FOLD - 1], resid[v, a, 0])
            face = jnp.sum(jnp.where(lane == column, face, 0.0), axis=1, keepdims=True)
            sums = sums + jnp.where(lane == slot + v * slots, face, 0.0)
    loop[...] = jnp.broadcast_to(jnp.sum(sums, axis=0, keepdims=True), loop.shape)


def coarse_kernel(
    own, below, above, u1, source, edges, sigma, tau,
    start, edge, one, one_edge, two, two_edge,
    u2s, r2s, s2, t2, f2, u3s, r3s, s3, t3, f3, buf2a, buf2b, buf3a, buf3b,
    n2, nf2, ns2, nt2, mid_a, mid_b,
):
    count = u1.shape[0]
    R, J = u1.shape[-2:]
    sub = rows_of(R, J)

    for at in range(8 * count + 4):
        if at < 8 * count:
            kind, rest = divmod(at, 4 * count)
            v, ab = divmod(rest, 4)
            a, b = divmod(ab, 2)
            dst = (u2s, r2s)[kind].at[v, a, b]
        else:
            a, b = divmod(at - 8 * count, 2)
            dst = s2.at[a, b]
        for part, message in enumerate((own, above, below)):
            dst[part * R : (part + 1) * R] = message[at * R : (at + 1) * R]

    for a in range(2):
        for b in range(2):
            t2[a, b] = step_size(s2[a, b], 0.25)
            res = residual(u2s, r2s, 1.0 + s2[a, b], 0.25, a, b, 2, 3 * R)
            for v in range(count):
                f2[v, a, b] = 2.0 * r2s[v, a, b] - res[v]
    first_section(buf2a, u2s, r2s, t2, 1.0 / SECTIONS2, 2)
    src, dst = buf2a, buf2b
    for k in range(1, SECTIONS2):
        section(dst, src, u2s, f2, s2, t2, 0.25, 1.0 / (SECTIONS2 - k), 2, 3 * R)
        src, dst = dst, src
    u2, r2 = src, dst
    for a in range(2):
        for b in range(2):
            res = residual(u2, f2, 1.0 + s2[a, b], 0.25, a, b, 2, 3 * R)
            for v in range(count):
                r2[v, a, b] = res[v]
    for v in range(count):
        u3s[v, 0, 0] = quarter(lambda i, j: u2[v, i, j])
        r3s[v, 0, 0] = quarter(lambda i, j: r2[v, i, j])
    s3[0, 0] = quarter(lambda i, j: s2[i, j])
    t3[0, 0] = step_size(s3[0, 0], 0.0625)

    res = residual(u3s, r3s, 0.25 + s3[0, 0], 0.0625, 0, 0, 1, 3 * R)
    for v in range(count):
        f3[v, 0, 0] = 2.0 * r3s[v, 0, 0] - res[v]
    first_section(buf3a, u3s, r3s, t3, 1.0 / SECTIONS3, 1)
    src3, dst3 = buf3a, buf3b
    for k in range(1, SECTIONS3):
        section(dst3, src3, u3s, f3, s3, t3, 0.0625, 1.0 / (SECTIONS3 - k), 1, 3 * R)
        src3, dst3 = dst3, src3

    def narrow(x):
        return x[:R], jnp.where(sub < R // 2, x[R : 2 * R], x[2 * R :])

    for v in range(count):
        gain = narrow(src3[v, 0, 0] - u3s[v, 0, 0])
        for a in range(2):
            for b in range(2):
                for part in range(2):
                    at = slice(part * R, (part + 1) * R)
                    n2[v, a, b, at] = narrow(u2[v, a, b])[part] + gain[part]
                    nf2[v, a, b, at] = narrow(f2[v, a, b])[part]
                    if v == 0:
                        ns2[a, b, at] = narrow(s2[a, b])[part]
                        nt2[a, b, at] = narrow(t2[a, b])[part]
    src = n2
    for k in range(SECTIONS2):
        dst = (mid_a, mid_b)[k % 2]
        section(dst, src, n2, nf2, ns2, nt2, 0.25, 1.0 / (SECTIONS2 - k), 2, 2 * R)
        src = dst

    first = (2 * count + 1) * 4 * R
    for v in range(count):
        for b in range(2):
            rim = {}
            for a in range(2):
                x, after = u2s[v, a, b], src[v, a, b]
                gain = after[:R] - x[:R]
                rim[0, a] = src[v, a, b, 2 * R - 1 :] - u2s[v, a, b, 3 * R - 1 :]
                rim[1, a] = src[v, a, b, R : R + 1] - u2s[v, a, b, R : R + 1]
                for i in range(2):
                    for j in range(2):
                        at = (v, 2 * a + i, 2 * b + j)
                        start[at] = u1[at] + gain
            lower = jnp.where(sub < FOLD // 2, rim[0, 0], rim[0, 1])
            upper = jnp.where(sub < FOLD + FOLD // 2, rim[1, 0], rim[1, 1])
            gain = jnp.where(sub < FOLD, lower, upper)
            for j in range(2):
                tile = edge.at[v, 2 * b + j]
                tile[...] = jnp.zeros((R, J), jnp.float32)
                at = first + (v * FOLD + 2 * b + j) * SECTIONS1
                tile[FOLD - SECTIONS1 : FOLD] = below[at : at + SECTIONS1]
                tile[FOLD : FOLD + SECTIONS1] = above[at : at + SECTIONS1]
                tile[...] = tile[...] + gain
    source_edge = edges.at[count : 2 * count]
    src, src_edge = start, edge
    for k, (dst, dst_edge) in enumerate(((one, one_edge), (two, two_edge))):
        fine_section(
            dst, dst_edge, src, src_edge, start, edge, source, source_edge, sigma, tau,
            1.0 / (SECTIONS1 - k),
        )
        src, src_edge = dst, dst_edge


def fine_kernel(
    start, edge, one, one_edge, two, two_edge, source, edges, sigma, tau, cells, loop, weight_ref,
    offset_ref,
    solution_ref, loop_out,
    patch, patch_edge, buf_a, buf_b, edge_a, edge_b, corr_ref, stage,
):
    count = start.shape[0]
    R, J = start.shape[-2:]
    N = corr_ref.shape[1]
    row = lax.axis_index("row")
    blk = lax.axis_index("blk")
    blocks = lax.axis_size("blk")
    slots = N // blocks
    wide = loop.shape[1]
    offset = offset_ref[0]
    shift = lax.rem(jnp.where(row == 0, N - offset, offset), N)
    both = []
    for r in range(2):
        held = loop[r * blocks : (r + 1) * blocks]
        for v in range(count):
            for c in range(0, N, wide):
                cell = lanes_of(blocks, wide) + c
                value = pick(held, cell // blocks + v * slots)
                value = jnp.where(wrap(cell, blocks) == rows_of(blocks, wide), value, 0.0)
                corr_ref[v : v + 1, c : c + wide] = jnp.sum(value, axis=0, keepdims=True)
        both.append(corr_ref[...])
    mine = jnp.where(row == 0, both[0], both[1])
    others = jnp.where(row == 0, both[1], both[0])
    correction = weight_ref[...] * (mine + pltpu.roll(others, shift, 1))
    corr_ref[...] = correction
    length = loop_out.shape[2]
    shown = pltpu.roll(correction, lax.rem(N - blk * length, N), 1)
    for v in range(count):
        loop_out[v] = shown[v : v + 1, :length]

    lane = lanes_of(R, J)
    ring = lanes_of(R, N)
    source_edge = edges.at[count : 2 * count]

    def smooth(side):
        face, column = ((FOLD - 1, J - 1), (0, 0))[side]
        for a in range(FOLD + 1):
            match = cells[a, :, :1] == ring
            for v in range(count):
                fix = jnp.where(match, corr_ref[v : v + 1], 0.0)
                fix = jnp.where(lane == column, jnp.sum(fix, axis=1, keepdims=True), 0.0)
                if a == FOLD:
                    patch_edge[v, face] = edge[v, face] + fix
                else:
                    patch[v, a, face] = start[v, a, face] + fix
        first = Mixed(start, patch, (face,), 2)
        first_edge = Mixed(edge, patch_edge, (face,), 1)
        src, src_edge = first, first_edge
        plain = ((one, one_edge), (two, two_edge), (None, None))
        fresh = ((buf_a, edge_a), (buf_b, edge_b), (buf_a, None))
        for k in range(SECTIONS1):
            groups = [b for b in range(FOLD) if abs(b - face) <= k + 1 or k == SECTIONS1 - 1]
            dst, dst_edge = fresh[k]
            fine_section(
                dst, dst_edge, src, src_edge, first, first_edge, source, source_edge, sigma, tau,
                1.0 / (SECTIONS1 - k), groups,
            )
            if k < SECTIONS1 - 1:
                src = Mixed(plain[k][0], dst, groups, 2)
                src_edge = Mixed(plain[k][1], dst_edge, groups, 1)

    for side in range(2):
        pl.when(row == side)(functools.partial(smooth, side))
    src = buf_a
    for v in range(count):
        for a in range(FOLD):
            for b in range(FOLD):
                stage[v, b, pl.ds(a, R, stride=FOLD), :] = src[v, a, b]
        for c, x in enumerate(join_lanes([stage[v, b] for b in range(FOLD)])):
            solution_ref[0, v, :, c * J : (c + 1) * J] = x


def body(state, forcing, sigma, partner, loop_weight, offset):
    _, count, rows, cols = state.shape
    R, J = rows // FOLD, cols // FOLD
    N = loop_weight.shape[1]
    blocks = lax.axis_size("blk")
    length = N // blocks
    real = functools.partial(jax.ShapeDtypeStruct, dtype=jnp.float32)
    near = lambda shape, dtype=jnp.float32: pltpu.VMEM(shape, dtype)
    away = lambda x: pltpu.with_memory_space_constraint(x, pltpu.HBM)
    held = lambda x: pltpu.with_memory_space_constraint(x, pltpu.VMEM)
    scratch = lambda *shape: pltpu.VMEM(shape, jnp.float32)
    far = pl.BlockSpec(memory_space=pltpu.HBM)
    deep = 2 * FOLD
    slots = partner[:, :, 0]
    packed = near((-(-(edge_rows(count)[1] + 1) // 8) * 8, cols))
    limit = pltpu.CompilerParams(vmem_limit_bytes=LIMIT)
    head, tail, s_near, f_near, g_near, p_near, w_near = pl.pallas_call(
        pack_kernel,
        in_specs=[far] * 5,
        out_specs=[vmem()] * 7,
        out_shape=[
            packed,
            packed,
            near((count, rows, cols)),
            near((count, rows, cols)),
            near((rows, cols)),
            near((1, rows), jnp.int32),
            near((1, N)),
        ],
        scratch_shapes=[pltpu.SemaphoreType.DMA((5,))],
        compiler_params=limit,
        name="pack",
    )(away(state), away(forcing), away(sigma), away(slots), away(loop_weight))
    up = [(i, (i + 1) % blocks) for i in range(blocks)]
    down = [((i + 1) % blocks, i) for i in range(blocks)]
    below = lax.ppermute(tail, "blk", up)
    above = lax.ppermute(head, "blk", down)

    st, fo, sg, own_slot = pl.pallas_call(
        fold_kernel,
        in_specs=[vmem()] * 4,
        out_specs=[vmem()] * 4,
        out_shape=[
            near((count, FOLD, FOLD, R, J)),
            near((count, FOLD, FOLD, R, J)),
            near((FOLD, FOLD, R, J)),
            near((FOLD, R, J), jnp.int32),
        ],
        scratch_shapes=[
            scratch(2 * count + 1, FOLD, rows, J),
            pltpu.VMEM((rows, J), jnp.int32),
        ],
        compiler_params=limit,
        name="fold",
    )(held(s_near), held(f_near), held(g_near), held(p_near))

    far_rows = (2 * count + 1) * 4 * R + count * SECTIONS1 * FOLD
    message = near((-(-far_rows // 8) * 8, J))
    fine = (count, FOLD, FOLD, R, J)
    rim = (count, FOLD, R, J)
    u1, edges, sigma_w, tau, cells, head, tail, loop = pl.pallas_call(
        down_kernel,
        in_specs=[vmem()] * 6,
        out_specs=[vmem()] * 8,
        out_shape=[
            near(fine),
            near((2 * count + 1, FOLD, R, J)),
            near((FOLD + 1, FOLD, R, J)),
            near((FOLD + 1, FOLD, R, J)),
            near((FOLD + 1, R, J), jnp.int32),
            message,
            message,
            near((2 * blocks, J)),
        ],
        scratch_shapes=[
            scratch(*fine),
            scratch(*fine),
            scratch(*rim),
            scratch(*rim),
            scratch(2 * FOLD, cols),
            scratch(*fine),
            scratch(8, length),
        ],
        compiler_params=limit,
        name="down",
    )(held(st), held(fo), held(sg), held(own_slot), held(below), held(above))

    below = lax.ppermute(tail, "blk", up)
    above = lax.ppermute(head, "blk", down)
    loop = lax.all_to_all(loop, ("row", "blk"), 0, 0, tiled=True)

    mid = (count, 2, 2, 3 * R, J)
    low = (count, 1, 1, 3 * R, J)
    thin = (count, 2, 2, 2 * R, J)
    states = pl.pallas_call(
        coarse_kernel,
        in_specs=[vmem()] * 8,
        out_specs=[vmem()] * 6,
        out_shape=[near(fine), near(rim)] * 3,
        scratch_shapes=[
            scratch(*mid), scratch(*mid), scratch(*mid[1:]), scratch(*mid[1:]), scratch(*mid),
            scratch(*low), scratch(*low), scratch(*low[1:]), scratch(*low[1:]), scratch(*low),
            scratch(*mid), scratch(*mid), scratch(*low), scratch(*low),
            scratch(*thin), scratch(*thin), scratch(*thin[1:]), scratch(*thin[1:]),
            scratch(*thin), scratch(*thin),
        ],
        compiler_params=limit,
        name="coarse",
    )(
        held(head), held(below), held(above), held(u1), held(fo), held(edges), held(sigma_w),
        held(tau),
    )
    result, loop_out = pl.pallas_call(
        fine_kernel,
        in_specs=[vmem()] * 13 + [pl.BlockSpec(memory_space=pltpu.SMEM)],
        out_specs=[vmem()] * 2,
        out_shape=[real(state.shape), real((count, 1, length))],
        scratch_shapes=[
            scratch(*fine), scratch(*rim),
            scratch(*fine), scratch(*fine), scratch(*rim), scratch(*rim),
            scratch(8, N),
            scratch(count, FOLD, rows, J),
        ],
        compiler_params=limit,
        name="fine",
    )(
        *[held(x) for x in states], held(fo), held(edges), held(sigma_w), held(tau), held(cells),
        held(loop), held(w_near), offset,
    )
    return result, jnp.transpose(loop_out, (1, 0, 2))


def solution(mesh):
    placed = (
        P("row", None, "blk", None),
        P("row", None, "blk", None),
        P("row", "blk", None),
        P("row", "blk", None),
        P("row", None),
        P(),
    )

    return jax.shard_map(
        body,
        mesh=mesh,
        in_specs=placed,
        out_specs=(P("row", None, "blk", None), P("row", None, "blk")),
        check_vma=False,
    )
```

```python
import functools

import jax
import jax.numpy as jnp
from jax import lax
from jax.experimental import pallas as pl
from jax.experimental.pallas import tpu as pltpu
from jax.sharding import PartitionSpec as P


SECTIONS1 = 3
SECTIONS2 = 3
SECTIONS3 = 4
COEFF = 0.8

FOLD = 4
LIMIT = 24 * 1024 * 1024


def vmem():
    return pl.BlockSpec(memory_space=pltpu.VMEM)


def lanes_of(rows, cols):
    return lax.broadcasted_iota(jnp.int32, (rows, cols), 1)


def rows_of(rows, cols):
    return lax.broadcasted_iota(jnp.int32, (rows, cols), 0)


def pick(x, index):
    return jnp.take_along_axis(x, index, axis=1, mode="promise_in_bounds")


def split_lanes(x):
    rows, cols = x.shape
    wide = cols // FOLD
    run = wide // FOLD
    lane = lanes_of(rows, wide)
    parts = [x[:, c * wide : (c + 1) * wide] for c in range(FOLD)]
    group = lane // run
    out = []
    for b in range(FOLD):
        index = (lane % run) * FOLD + b
        taken = [pick(p, index) for p in parts]
        value = taken[-1]
        for c in range(FOLD - 1):
            value = jnp.where(group == c, taken[c], value)
        out.append(value)
    return out


def join_lanes(parts, blocks=range(FOLD)):
    rows, wide = parts[0].shape
    run = wide // FOLD
    lane = lanes_of(rows, wide)
    turn = lane % FOLD
    out = []
    for c in blocks:
        index = lane // FOLD + c * run
        taken = [pick(p, index) for p in parts]
        value = taken[-1]
        for b in range(FOLD - 1):
            value = jnp.where(turn == b, taken[b], value)
        out.append(value)
    return out


def joined(tiles, stage, v, blocks=range(FOLD)):
    R = tiles.shape[-2]
    for a in range(FOLD):
        for b in range(FOLD):
            stage[v, b, pl.ds(a, R, stride=FOLD), :] = tiles[v, a, b]
    return join_lanes([stage[v, b] for b in range(FOLD)], blocks)


def residual(src, source, diag, scale, a, b, fold, rows):
    count = src.shape[0]
    total, wide = src.shape[-2:]
    u = [src[v, a, b][:rows] for v in range(count)]
    q = u[0] * u[0]
    for v in range(1, count):
        q = q + u[v] * u[v]
    q = q * (1.0 / count)
    factor = diag + 0.5 * q / (1.0 + q)
    lane = lanes_of(rows, wide)
    out = []
    for v in range(count):
        up = src[v, a - 1, b] if a else pltpu.roll(src[v, fold - 1, b], 1, 0)
        down = src[v, a + 1, b] if a < fold - 1 else pltpu.roll(src[v, 0, b], total - 1, 0)
        if b:
            left = src[v, a, b - 1][:rows]
        else:
            left = jnp.where(lane == 0, 0.0, pltpu.roll(src[v, a, fold - 1][:rows], 1, 1))
        if b < fold - 1:
            right = src[v, a, b + 1][:rows]
        else:
            right = jnp.where(lane == wide - 1, 0.0, pltpu.roll(src[v, a, 0][:rows], wide - 1, 1))
        near = (up[:rows] + down[:rows]) + (left + right)
        out.append(source[v, a, b][:rows] + scale * near - factor * u[v])
    return out


def section(dst, src, start, source, sigma, tau, scale, weight, fold, rows):
    for a in range(fold):
        for b in range(fold):
            diag = 4.0 * scale + sigma[a, b][:rows]
            step = weight * tau[a, b][:rows]
            res = residual(src, source, diag, scale, a, b, fold, rows)
            for v, r in enumerate(res):
                dst[v, a, b, :rows] = start[v, a, b][:rows] + step * r


def first_section(dst, start, coarse, tau, weight, fold):
    for a in range(fold):
        for b in range(fold):
            step = weight * tau[a, b]
            for v in range(dst.shape[0]):
                dst[v, a, b] = start[v, a, b] + step * coarse[v, a, b]


def step_size(sigma, scale):
    return COEFF / (4.0 * scale + sigma + 1.5)


def fine_residual(src, edge, source, diag, b, a=None):
    count = src.shape[0]
    R, J = src.shape[-2:]
    sub, lane = rows_of(R, J), lanes_of(R, J)
    top = FOLD - 1
    at = (lambda v, i: edge[v, i]) if a is None else (lambda v, i: src[v, a, i])
    u = [at(v, b) for v in range(count)]
    q = u[0] * u[0]
    for v in range(1, count):
        q = q + u[v] * u[v]
    q = q * (1.0 / count)
    factor = diag + 0.5 * q / (1.0 + q)
    out = []
    for v in range(count):
        if a is None:
            up = jnp.where(sub == FOLD, src[v, top, b, R - 1 :], pltpu.roll(u[v], 1, 0))
            down = jnp.where(sub == top, src[v, 0, b, :1], pltpu.roll(u[v], R - 1, 0))
        else:
            if a:
                up = src[v, a - 1, b]
            else:
                up = jnp.where(sub == 0, edge[v, b, top : top + 1], pltpu.roll(src[v, top, b], 1, 0))
            if a < top:
                down = src[v, a + 1, b]
            else:
                below = edge[v, b, FOLD : FOLD + 1]
                down = jnp.where(sub == R - 1, below, pltpu.roll(src[v, 0, b], R - 1, 0))
        left = at(v, b - 1) if b else jnp.where(lane == 0, 0.0, pltpu.roll(at(v, top), 1, 1))
        right = at(v, b + 1) if b < top else jnp.where(lane == J - 1, 0.0, pltpu.roll(at(v, 0), J - 1, 1))
        near = (up + down) + (left + right)
        out.append((source[v, b] if a is None else source[v, a, b]) + near - factor * u[v])
    return out


def fine_section(dst, dst_edge, src, edge, start, start_edge, source, source_edge, sigma, tau, weight,
                 groups=range(FOLD)):
    for a in range(FOLD + 1):
        if a == FOLD and dst_edge is None:
            continue
        for b in groups:
            diag = 4.0 + sigma[a, b]
            step = weight * tau[a, b]
            if a == FOLD:
                res = fine_residual(src, edge, source_edge, diag, b)
            else:
                res = fine_residual(src, edge, source, diag, b, a)
            for v, r in enumerate(res):
                if a == FOLD:
                    dst_edge[v, b] = start_edge[v, b] + step * r
                else:
                    dst[v, a, b] = start[v, a, b] + step * r


class Mixed:
    def __init__(self, base, fresh, groups, axis):
        self.base, self.fresh, self.groups, self.axis = base, fresh, groups, axis
        self.shape = base.shape

    def __getitem__(self, at):
        return (self.fresh if at[self.axis] in self.groups else self.base)[at]


def quarter(x):
    return 0.25 * ((x(0, 0) + x(0, 1)) + (x(1, 0) + x(1, 1)))


def wrap(x, size):
    return x & (size - 1) if size & (size - 1) == 0 else lax.rem(x, size)


def fetch(pairs, sems):
    copies = [pltpu.make_async_copy(x, y, sems.at[k]) for k, (x, y) in enumerate(pairs)]
    for copy in copies:
        copy.start()
    for copy in copies:
        copy.wait()


def edge_rows(count):
    out = []
    at = 0
    for kind, width in ((0, SECTIONS1 + 1), (1, SECTIONS1), (2, SECTIONS1)):
        for v in range(1 if kind == 2 else count):
            out.append((kind, v, at, width))
            at += width
    return out, at


def pack_kernel(
    s_hbm, f_hbm, g_hbm, p_hbm, w_hbm, head, tail, s_ref, f_ref, g_ref, p_ref, w_ref, sems
):
    count, rows = s_ref.shape[:2]
    fetch(
        (
            (p_hbm, p_ref), (w_hbm, w_ref), (s_hbm.at[0], s_ref), (f_hbm.at[0], f_ref),
            (g_hbm.at[0], g_ref),
        ),
        sems,
    )
    places, end = edge_rows(count)
    for kind, v, at, width in places:
        x = g_ref if kind == 2 else (s_ref, f_ref)[kind].at[v]
        head[at : at + width] = x[:width]
        tail[at : at + width] = x[rows - width :]
    for message in (head, tail):
        message[end:] = jnp.zeros((message.shape[0] - end, message.shape[1]), jnp.float32)
        message[end : end + 1, :rows] = p_ref[...].astype(jnp.float32)


def fold_kernel(s_ref, f_ref, g_ref, p_ref, st, fo, sg, own_slot, stage, slots):
    count = st.shape[0]
    R, _ = st.shape[-2:]
    rows = s_ref.shape[1]
    for ch in range(2 * count + 1):
        kind, v = divmod(ch, count)
        x = g_ref[...] if kind == 2 else (s_ref, f_ref)[kind][v]
        for b, part in enumerate(split_lanes(x)):
            stage[ch, b] = part
        for a in range(FOLD):
            for b in range(FOLD):
                part = stage[ch, b, pl.ds(a, R, stride=FOLD), :]
                if kind == 2:
                    sg[a, b] = part
                else:
                    (st, fo)[kind][v, a, b] = part
    diagonal = lanes_of(rows, rows) == rows_of(rows, rows)
    column = jnp.where(diagonal, p_ref[...].astype(jnp.float32), 0.0)
    column = jnp.sum(column, axis=1, keepdims=True).astype(jnp.int32)
    slots[...] = jnp.broadcast_to(column, slots.shape)
    for a in range(FOLD):
        own_slot[a] = slots[pl.ds(a, R, stride=FOLD), :]


def down_kernel(
    st, fo, sg, own_slot, below, above,
    u1, edges, sigma, tau, cells, head, tail, loop,
    buf_a, buf_b, edge_a, edge_b, box, resid, own_loop,
):
    count = st.shape[0]
    R, J = st.shape[-2:]
    row = lax.axis_index("row")
    blk = lax.axis_index("blk")
    blocks = lax.axis_size("blk")
    slots = own_loop.shape[1]
    N = blocks * slots
    rows = R * FOLD
    sub = rows_of(R, J)
    places, end = edge_rows(count)
    for ch, (kind, v, at, width) in enumerate(places):
        if width < FOLD:
            box[...] = jnp.zeros_like(box)
        box[FOLD - width : FOLD] = below[at : at + width]
        box[FOLD : FOLD + width] = above[at : at + width]
        for b, part in enumerate(split_lanes(box[...])):
            edges[ch, b] = part
    for b in range(FOLD):
        for a in range(FOLD):
            sigma[a, b] = sg[a, b]
            tau[a, b] = step_size(sg[a, b], 1.0)
        sigma[FOLD, b] = edges[2 * count, b]
        tau[FOLD, b] = step_size(edges[2 * count, b], 1.0)

    place = lanes_of(1, rows)
    high = lax.rem(blk + 1, blocks)
    low = lax.rem(blk + blocks - 1, blocks)
    column = jnp.zeros((R, J), jnp.int32)
    for k in range(2 * FOLD):
        message, i = (below, rows - FOLD + k) if k < FOLD else (above, k - FOLD)
        x = jnp.where(place == i, message[end : end + 1, :rows], 0.0)
        x = jnp.sum(x, axis=1, keepdims=True).astype(jnp.int32)
        column = jnp.where(sub == k, jnp.broadcast_to(x, (R, J)), column)
    cells[FOLD] = wrap(column * blocks + jnp.where(sub < FOLD, low, high), N)
    for a in range(FOLD):
        cells[a] = wrap(own_slot[a] * blocks + blk, N)

    start_edge = edges.at[:count]
    source_edge = edges.at[count : 2 * count]
    src, edge = st, start_edge
    for k in range(SECTIONS1):
        dst = u1 if k == SECTIONS1 - 1 else (buf_a, buf_b)[k % 2]
        dst_edge = (edge_a, edge_b)[k % 2]
        fine_section(
            dst, dst_edge, src, edge, st, start_edge, fo, source_edge, sigma, tau, 1.0 / (SECTIONS1 - k)
        )
        src, edge = dst, dst_edge

    first = (2 * count + 1) * 4 * R
    for a in range(FOLD):
        for b in range(FOLD):
            res = fine_residual(u1, edge, fo, 4.0 + sigma[a, b], b, a)
            for v in range(count):
                resid[v, a, b] = res[v]
                at = first + (v * FOLD + b) * SECTIONS1 + a
                if a < SECTIONS1:
                    head[at : at + 1] = u1[v, a, b, :1]
                at -= FOLD - SECTIONS1
                if a >= FOLD - SECTIONS1:
                    tail[at : at + 1] = u1[v, a, b, R - 1 :]
    for a in range(2):
        for b in range(2):
            for v in range(count):
                at = ((v * 2 + a) * 2 + b) * R
                x = quarter(lambda i, j: u1[v, 2 * a + i, 2 * b + j])
                head[at : at + R] = x
                tail[at : at + R] = x
                at += 4 * count * R
                x = quarter(lambda i, j: resid[v, 2 * a + i, 2 * b + j])
                head[at : at + R] = x
                tail[at : at + R] = x
            at = (8 * count + a * 2 + b) * R
            x = quarter(lambda i, j: sg[2 * a + i, 2 * b + j])
            head[at : at + R] = x
            tail[at : at + R] = x

    lane = lanes_of(R, J)
    column = jnp.where(row == 0, J - 1, 0)
    sums = jnp.zeros((R, J), jnp.float32)
    for a in range(FOLD):
        slot = wrap(own_slot[a], slots)
        for v in range(count):
            face = jnp.where(row == 0, resid[v, a, FOLD - 1], resid[v, a, 0])
            face = jnp.sum(jnp.where(lane == column, face, 0.0), axis=1, keepdims=True)
            sums = sums + jnp.where(lane == slot + v * slots, face, 0.0)
    loop[...] = jnp.broadcast_to(jnp.sum(sums, axis=0, keepdims=True), loop.shape)


def coarse_kernel(
    own, below, above, u1, source, edges, sigma, tau,
    start, edge, one, one_edge, two, two_edge, solution_hbm,
    u2s, r2s, s2, t2, f2, u3s, r3s, s3, t3, f3, buf2a, buf2b, buf3a, buf3b,
    n2, nf2, ns2, nt2, mid_a, mid_b, three, stage, solution_ref, sems,
):
    count = u1.shape[0]
    R, J = u1.shape[-2:]
    sub = rows_of(R, J)

    for at in range(8 * count + 4):
        if at < 8 * count:
            kind, rest = divmod(at, 4 * count)
            v, ab = divmod(rest, 4)
            a, b = divmod(ab, 2)
            dst = (u2s, r2s)[kind].at[v, a, b]
        else:
            a, b = divmod(at - 8 * count, 2)
            dst = s2.at[a, b]
        for part, message in enumerate((own, above, below)):
            dst[part * R : (part + 1) * R] = message[at * R : (at + 1) * R]

    for a in range(2):
        for b in range(2):
            t2[a, b] = step_size(s2[a, b], 0.25)
            res = residual(u2s, r2s, 1.0 + s2[a, b], 0.25, a, b, 2, 3 * R)
            for v in range(count):
                f2[v, a, b] = 2.0 * r2s[v, a, b] - res[v]
    first_section(buf2a, u2s, r2s, t2, 1.0 / SECTIONS2, 2)
    src, dst = buf2a, buf2b
    for k in range(1, SECTIONS2):
        section(dst, src, u2s, f2, s2, t2, 0.25, 1.0 / (SECTIONS2 - k), 2, 3 * R)
        src, dst = dst, src
    u2, r2 = src, dst
    for a in range(2):
        for b in range(2):
            res = residual(u2, f2, 1.0 + s2[a, b], 0.25, a, b, 2, 3 * R)
            for v in range(count):
                r2[v, a, b] = res[v]
    for v in range(count):
        u3s[v, 0, 0] = quarter(lambda i, j: u2[v, i, j])
        r3s[v, 0, 0] = quarter(lambda i, j: r2[v, i, j])
    s3[0, 0] = quarter(lambda i, j: s2[i, j])
    t3[0, 0] = step_size(s3[0, 0], 0.0625)

    res = residual(u3s, r3s, 0.25 + s3[0, 0], 0.0625, 0, 0, 1, 3 * R)
    for v in range(count):
        f3[v, 0, 0] = 2.0 * r3s[v, 0, 0] - res[v]
    first_section(buf3a, u3s, r3s, t3, 1.0 / SECTIONS3, 1)
    src3, dst3 = buf3a, buf3b
    for k in range(1, SECTIONS3):
        section(dst3, src3, u3s, f3, s3, t3, 0.0625, 1.0 / (SECTIONS3 - k), 1, 3 * R)
        src3, dst3 = dst3, src3

    def narrow(x):
        return x[:R], jnp.where(sub < R // 2, x[R : 2 * R], x[2 * R :])

    for v in range(count):
        gain = narrow(src3[v, 0, 0] - u3s[v, 0, 0])
        for a in range(2):
            for b in range(2):
                for part in range(2):
                    at = slice(part * R, (part + 1) * R)
                    n2[v, a, b, at] = narrow(u2[v, a, b])[part] + gain[part]
                    nf2[v, a, b, at] = narrow(f2[v, a, b])[part]
                    if v == 0:
                        ns2[a, b, at] = narrow(s2[a, b])[part]
                        nt2[a, b, at] = narrow(t2[a, b])[part]
    src = n2
    for k in range(SECTIONS2):
        dst = (mid_a, mid_b)[k % 2]
        section(dst, src, n2, nf2, ns2, nt2, 0.25, 1.0 / (SECTIONS2 - k), 2, 2 * R)
        src = dst

    first = (2 * count + 1) * 4 * R
    for v in range(count):
        for b in range(2):
            rim = {}
            for a in range(2):
                x, after = u2s[v, a, b], src[v, a, b]
                gain = after[:R] - x[:R]
                rim[0, a] = src[v, a, b, 2 * R - 1 :] - u2s[v, a, b, 3 * R - 1 :]
                rim[1, a] = src[v, a, b, R : R + 1] - u2s[v, a, b, R : R + 1]
                for i in range(2):
                    for j in range(2):
                        at = (v, 2 * a + i, 2 * b + j)
                        start[at] = u1[at] + gain
            lower = jnp.where(sub < FOLD // 2, rim[0, 0], rim[0, 1])
            upper = jnp.where(sub < FOLD + FOLD // 2, rim[1, 0], rim[1, 1])
            gain = jnp.where(sub < FOLD, lower, upper)
            for j in range(2):
                tile = edge.at[v, 2 * b + j]
                tile[...] = jnp.zeros((R, J), jnp.float32)
                at = first + (v * FOLD + 2 * b + j) * SECTIONS1
                tile[FOLD - SECTIONS1 : FOLD] = below[at : at + SECTIONS1]
                tile[FOLD : FOLD + SECTIONS1] = above[at : at + SECTIONS1]
                tile[...] = tile[...] + gain
    source_edge = edges.at[count : 2 * count]
    src, src_edge = start, edge
    for k, (dst, dst_edge) in enumerate(((one, one_edge), (two, two_edge), (three, None))):
        fine_section(
            dst, dst_edge, src, src_edge, start, edge, source, source_edge, sigma, tau,
            1.0 / (SECTIONS1 - k),
        )
        src, src_edge = dst, dst_edge
    copies = []
    for v in range(count):
        for c, x in enumerate(joined(three, stage, v)):
            solution_ref[v, :, c * J : (c + 1) * J] = x
        copies.append(pltpu.make_async_copy(solution_ref.at[v], solution_hbm.at[0, v], sems.at[v]))
        copies[-1].start()
    for copy in copies:
        copy.wait()


def fine_kernel(
    start, edge, one, one_edge, two, two_edge, source, edges, sigma, tau, cells, loop, weight_ref,
    offset_ref, old_hbm,
    solution_hbm, loop_hbm,
    patch, patch_edge, buf_a, buf_b, edge_a, edge_b, corr_ref, stage, strip, sem,
    loop_out, loop_sem,
):
    count = start.shape[0]
    R, J = start.shape[-2:]
    N = corr_ref.shape[1]
    row = lax.axis_index("row")
    blk = lax.axis_index("blk")
    blocks = lax.axis_size("blk")
    slots = N // blocks
    wide = loop.shape[1]
    offset = offset_ref[0]
    shift = lax.rem(jnp.where(row == 0, N - offset, offset), N)
    both = []
    for r in range(2):
        held = loop[r * blocks : (r + 1) * blocks]
        for v in range(count):
            for c in range(0, N, wide):
                cell = lanes_of(blocks, wide) + c
                value = pick(held, cell // blocks + v * slots)
                value = jnp.where(wrap(cell, blocks) == rows_of(blocks, wide), value, 0.0)
                corr_ref[v : v + 1, c : c + wide] = jnp.sum(value, axis=0, keepdims=True)
        both.append(corr_ref[...])
    mine = jnp.where(row == 0, both[0], both[1])
    others = jnp.where(row == 0, both[1], both[0])
    correction = weight_ref[...] * (mine + pltpu.roll(others, shift, 1))
    corr_ref[...] = correction
    length = loop_out.shape[2]
    shown = pltpu.roll(correction, lax.rem(N - blk * length, N), 1)
    for v in range(count):
        loop_out[v] = shown[v : v + 1, :length]
    loop_copy = pltpu.make_async_copy(loop_out, loop_hbm, loop_sem)
    loop_copy.start()

    lane = lanes_of(R, J)
    ring = lanes_of(R, N)
    source_edge = edges.at[count : 2 * count]

    def smooth(side):
        face, column = ((FOLD - 1, J - 1), (0, 0))[side]
        for a in range(FOLD + 1):
            match = cells[a, :, :1] == ring
            for v in range(count):
                fix = jnp.where(match, corr_ref[v : v + 1], 0.0)
                fix = jnp.where(lane == column, jnp.sum(fix, axis=1, keepdims=True), 0.0)
                if a == FOLD:
                    patch_edge[v, face] = edge[v, face] + fix
                else:
                    patch[v, a, face] = start[v, a, face] + fix
        first = Mixed(start, patch, (face,), 2)
        first_edge = Mixed(edge, patch_edge, (face,), 1)
        src, src_edge = first, first_edge
        plain = ((one, one_edge), (two, two_edge), (None, None))
        fresh = ((buf_a, edge_a), (buf_b, edge_b), (buf_a, None))
        for k in range(SECTIONS1):
            groups = [b for b in range(FOLD) if abs(b - face) <= k + 1 or k == SECTIONS1 - 1]
            dst, dst_edge = fresh[k]
            fine_section(
                dst, dst_edge, src, src_edge, first, first_edge, source, source_edge, sigma, tau,
                1.0 / (SECTIONS1 - k), groups,
            )
            if k < SECTIONS1 - 1:
                src = Mixed(plain[k][0], dst, groups, 2)
                src_edge = Mixed(plain[k][1], dst_edge, groups, 1)
        c = face
        for v in range(count):
            (strip[v],) = joined(buf_a, stage, v, (c,))
        copy = pltpu.make_async_copy(strip, solution_hbm.at[0, :, :, c * J : (c + 1) * J], sem)
        copy.start()
        copy.wait()

    for side in range(2):
        pl.when(row == side)(functools.partial(smooth, side))
    loop_copy.wait()


def body(state, forcing, sigma, partner, loop_weight, offset):
    _, count, rows, cols = state.shape
    R, J = rows // FOLD, cols // FOLD
    N = loop_weight.shape[1]
    blocks = lax.axis_size("blk")
    length = N // blocks
    near = lambda shape, dtype=jnp.float32: pltpu.VMEM(shape, dtype)
    away = lambda x: pltpu.with_memory_space_constraint(x, pltpu.HBM)
    held = lambda x: pltpu.with_memory_space_constraint(x, pltpu.VMEM)
    scratch = lambda *shape: pltpu.VMEM(shape, jnp.float32)
    far = pl.BlockSpec(memory_space=pltpu.HBM)
    deep = 2 * FOLD
    slots = partner[:, :, 0]
    packed = near((-(-(edge_rows(count)[1] + 1) // 8) * 8, cols))
    limit = pltpu.CompilerParams(vmem_limit_bytes=LIMIT)
    head, tail, s_near, f_near, g_near, p_near, w_near = pl.pallas_call(
        pack_kernel,
        in_specs=[far] * 5,
        out_specs=[vmem()] * 7,
        out_shape=[
            packed,
            packed,
            near((count, rows, cols)),
            near((count, rows, cols)),
            near((rows, cols)),
            near((1, rows), jnp.int32),
            near((1, N)),
        ],
        scratch_shapes=[pltpu.SemaphoreType.DMA((5,))],
        compiler_params=limit,
        name="pack",
    )(away(state), away(forcing), away(sigma), away(slots), away(loop_weight))
    up = [(i, (i + 1) % blocks) for i in range(blocks)]
    down = [((i + 1) % blocks, i) for i in range(blocks)]
    below = lax.ppermute(tail, "blk", up)
    above = lax.ppermute(head, "blk", down)

    st, fo, sg, own_slot = pl.pallas_call(
        fold_kernel,
        in_specs=[vmem()] * 4,
        out_specs=[vmem()] * 4,
        out_shape=[
            near((count, FOLD, FOLD, R, J)),
            near((count, FOLD, FOLD, R, J)),
            near((FOLD, FOLD, R, J)),
            near((FOLD, R, J), jnp.int32),
        ],
        scratch_shapes=[
            scratch(2 * count + 1, FOLD, rows, J),
            pltpu.VMEM((rows, J), jnp.int32),
        ],
        compiler_params=limit,
        name="fold",
    )(held(s_near), held(f_near), held(g_near), held(p_near))

    far_rows = (2 * count + 1) * 4 * R + count * SECTIONS1 * FOLD
    message = near((-(-far_rows // 8) * 8, J))
    fine = (count, FOLD, FOLD, R, J)
    rim = (count, FOLD, R, J)
    u1, edges, sigma_w, tau, cells, head, tail, loop = pl.pallas_call(
        down_kernel,
        in_specs=[vmem()] * 6,
        out_specs=[vmem()] * 8,
        out_shape=[
            near(fine),
            near((2 * count + 1, FOLD, R, J)),
            near((FOLD + 1, FOLD, R, J)),
            near((FOLD + 1, FOLD, R, J)),
            near((FOLD + 1, R, J), jnp.int32),
            message,
            message,
            near((2 * blocks, J)),
        ],
        scratch_shapes=[
            scratch(*fine),
            scratch(*fine),
            scratch(*rim),
            scratch(*rim),
            scratch(2 * FOLD, cols),
            scratch(*fine),
            scratch(8, length),
        ],
        compiler_params=limit,
        name="down",
    )(held(st), held(fo), held(sg), held(own_slot), held(below), held(above))

    below = lax.ppermute(tail, "blk", up)
    above = lax.ppermute(head, "blk", down)
    loop = lax.all_to_all(loop, ("row", "blk"), 0, 0, tiled=True)

    mid = (count, 2, 2, 3 * R, J)
    low = (count, 1, 1, 3 * R, J)
    thin = (count, 2, 2, 2 * R, J)
    *states, result = pl.pallas_call(
        coarse_kernel,
        in_specs=[vmem()] * 8,
        out_specs=[vmem()] * 6 + [far],
        out_shape=[near(fine), near(rim)] * 3 + [pltpu.HBM(state.shape, jnp.float32)],
        scratch_shapes=[
            scratch(*mid), scratch(*mid), scratch(*mid[1:]), scratch(*mid[1:]), scratch(*mid),
            scratch(*low), scratch(*low), scratch(*low[1:]), scratch(*low[1:]), scratch(*low),
            scratch(*mid), scratch(*mid), scratch(*low), scratch(*low),
            scratch(*thin), scratch(*thin), scratch(*thin[1:]), scratch(*thin[1:]),
            scratch(*thin), scratch(*thin),
            scratch(*fine),
            scratch(count, FOLD, rows, J),
            scratch(count, rows, cols),
            pltpu.SemaphoreType.DMA((count,)),
        ],
        compiler_params=limit,
        name="coarse",
    )(
        held(head), held(below), held(above), held(u1), held(fo), held(edges), held(sigma_w),
        held(tau),
    )
    result, loop_out = pl.pallas_call(
        fine_kernel,
        in_specs=[vmem()] * 13 + [pl.BlockSpec(memory_space=pltpu.SMEM), far],
        out_specs=[far, far],
        out_shape=[pltpu.HBM(state.shape, jnp.float32), pltpu.HBM((count, 1, length), jnp.float32)],
        input_output_aliases={14: 0},
        scratch_shapes=[
            scratch(*fine), scratch(*rim),
            scratch(*fine), scratch(*fine), scratch(*rim), scratch(*rim),
            scratch(8, N),
            scratch(count, FOLD, rows, J),
            scratch(count, rows, J),
            pltpu.SemaphoreType.DMA(()),
            scratch(count, 1, length),
            pltpu.SemaphoreType.DMA(()),
        ],
        compiler_params=limit,
        name="fine",
    )(
        *[held(x) for x in states], held(fo), held(edges), held(sigma_w), held(tau), held(cells),
        held(loop), held(w_near), offset, result,
    )
    return result, jnp.transpose(loop_out, (1, 0, 2))


def solution(mesh):
    placed = (
        P("row", None, "blk", None),
        P("row", None, "blk", None),
        P("row", "blk", None),
        P("row", "blk", None),
        P("row", None),
        P(),
    )

    return jax.shard_map(
        body,
        mesh=mesh,
        in_specs=placed,
        out_specs=(P("row", None, "blk", None), P("row", None, "blk")),
        check_vma=False,
    )
```
